32 devices in a mesh: gx: 2 (over x), gy: 4 (over y, core), gz: 4 (over z).
Axes of the slice: x: 2, y: 2, z: 4, core: 2. Of those that a mesh axis runs over, the one named last changes fastest.
Arguments:
- positions: float32 [3, 4, 8, 16, 128], P(None, 'gx', 'gy', 'gz'), may hold values from 0 to 1
- species: int32 [4, 8, 16, 128], P('gx', 'gy', 'gz'), may hold values from 0 to 1
- counts: int32 [4, 8, 16], P('gx', 'gy', 'gz'), may hold values from 0 to 128, as said below
Outputs:
- forces: float32 [3, 4, 8, 16, 128], P(None, 'gx', 'gy', 'gz')
- energy: float32 [4, 8, 16, 128], P('gx', 'gy', 'gz')
The draws below stay inside these ranges and needn't reach their ends.
Inputs may be any that keep to these rules, and one draw needn't show every extreme that they name: `counts`: slots at or beyond a tile's count are empty; tiles in the lower half of the surface normal are nearly full, those above it nearly empty except for a block of tiles holding the nanoparticle.
All inputs are finite; a program needn't handle non-finite values.
Results may differ from the reference program's by a relative error of at most 0.0001.
Values sent between devices are 32-bit elements; how exact they have to be, the bound alone decides.
No kernel may reach another device: no remote copies, remote signals or barrier semaphores. Data moves between devices by JAX's collectives and lax.ppermute only.
A program may use at most 64 MiB of HBM per device.

```python
import jax
import jax.numpy as jnp
from jax import lax

TILE = 128
NTX = 4
NTY = 8
NTZ = 16


def draw_counts(key, part):
    crowded_key, sparse_key = jax.random.split(jax.random.fold_in(key, 17))
    shape = (NTX, NTY, NTZ)
    crowded = jax.random.randint(crowded_key, shape, TILE * 3 // 4, TILE + 1)
    sparse = jax.random.randint(sparse_key, shape, 0, TILE // 8 + 1)
    position_x = lax.broadcasted_iota(jnp.int32, shape, 0)
    position_y = lax.broadcasted_iota(jnp.int32, shape, 1)
    height = lax.broadcasted_iota(jnp.int32, shape, 2)
    cluster = (height >= NTZ // 2) & (height < NTZ // 2 + 2) & (position_x < 2) & (position_y < 2)
    filled_tile = (height < NTZ // 2) | cluster
    return jnp.where(filled_tile, crowded, sparse).astype(jnp.int32)


def with_ends(drawn, stream_key, low, high):
    longest = drawn.shape.index(max(drawn.shape))
    spots = []
    for shift in (0, 1):
        where = [jax.random.randint(jax.random.fold_in(stream_key, axis), (), 0, length) for axis, length in enumerate(drawn.shape)]
        where[longest] = (where[longest] + shift) % drawn.shape[longest]
        spots.append(tuple(where))
    return drawn.at[spots[0]].set(low).at[spots[1]].set(high)


def block_scale(own_key, shape, pieces, least, top_value):
    factor_of = 1.0
    for dim, blocks in pieces:
        heights = jax.random.uniform(jax.random.fold_in(jax.random.fold_in(own_key, 6), dim), (blocks,), jnp.float32, least / len(pieces), top_value / len(pieces))
        factor_of = factor_of * jnp.repeat(jnp.exp(heights), shape[dim] // blocks).reshape((-1,) + (1,) * (len(shape) - 1 - dim))
    return factor_of


def setup_inputs(seed: int = 0) -> dict:
    keys = jax.random.split(jax.random.key(seed), 4)
    return {
        "positions": jnp.clip(1.0 * jax.random.uniform(keys[0], (3, NTX, NTY, NTZ, TILE), jnp.float32) ** block_scale(keys[0], (3, NTX, NTY, NTZ, TILE), ((1, 2), (2, 4), (3, 4)), -0.2, 0.2), 0.0, 1.0),
        "species": with_ends(jax.random.randint(keys[1], (NTX, NTY, NTZ, TILE), 0, 2), jax.random.fold_in(keys[1], 1), 0, 1).astype(jnp.int32),
        "counts": draw_counts(jax.random.fold_in(keys[3], 71), 0),
    }


CUTOFF_SQUARED = 0.2025
DENSITY_BASE = 1.0
DENSITY_STEP = 0.4
EMBED_BASE = 1.0
EMBED_STEP = -0.3
PAIR_BASE = 0.6
PAIR_STEP = 0.3

def neighbour_offsets():
    return [(first, second, third) for first in (-1, 0, 1) for second in (-1, 0, 1) for third in (-1, 0, 1)]

def kernels(squared):
    reach = jnp.maximum(1.0 - squared / CUTOFF_SQUARED, 0.0)
    reach_two = reach * reach
    return (reach_two * reach, reach_two * reach_two, -3.0 * reach_two / CUTOFF_SQUARED, -4.0 * reach_two * reach / CUTOFF_SQUARED)

def shifted(field, offset):
    extent_x = field.shape[-4] - 2
    extent_y = field.shape[-3] - 2
    extent_z = field.shape[-2] - 2
    return field[..., 1 + offset[0]:1 + offset[0] + extent_x, 1 + offset[1]:1 + offset[1] + extent_y, 1 + offset[2]:1 + offset[2] + extent_z, :]

def geometry(centre, beside, offset):
    parts = [beside[comp][..., None, :] + float(offset[comp]) - centre[comp][..., :, None] for comp in range(3)]
    squared = parts[0] * parts[0] + parts[1] * parts[1] + parts[2] * parts[2]
    return (parts, squared)

def densities(extended):
    centre = shifted(extended, (0, 0, 0))
    self_mask = 1.0 - jnp.eye(centre.shape[-1], dtype=jnp.float32)
    total = jnp.zeros(centre.shape[1:], jnp.float32)
    for offset in neighbour_offsets():
        beside = shifted(extended, offset)
        parts, squared = geometry(centre, beside, offset)
        cube = kernels(squared)[0]
        weight = beside[3] * (DENSITY_BASE + DENSITY_STEP * beside[4])
        terms = cube * weight[..., None, :]
        if offset == (0, 0, 0):
            terms = terms * self_mask
        total = total + lax.optimization_barrier(jnp.sum(terms, axis=-1))
    return total

def embedding(density, state):
    strength = state[3] * (EMBED_BASE + EMBED_STEP * state[4])
    root = jnp.sqrt(1.0 + density)
    return (-strength * root, -0.5 * strength / root)

def forces_of(extended, derivative_ext):
    centre = shifted(extended, (0, 0, 0))
    slope_own = shifted(derivative_ext, (0, 0, 0))
    dens_own = centre[3] * (DENSITY_BASE + DENSITY_STEP * centre[4])
    pair_own = centre[3] * (PAIR_BASE + PAIR_STEP * centre[4])
    self_mask = 1.0 - jnp.eye(centre.shape[-1], dtype=jnp.float32)
    total = jnp.zeros((3,) + centre.shape[1:], jnp.float32)
    pair_total = jnp.zeros(centre.shape[1:], jnp.float32)
    for offset in neighbour_offsets():
        beside = shifted(extended, offset)
        slope_beside = shifted(derivative_ext, offset)
        parts, squared = geometry(centre, beside, offset)
        cube, quart, cube_slope, quart_slope = kernels(squared)
        dens_beside = beside[3] * (DENSITY_BASE + DENSITY_STEP * beside[4])
        pair_beside = beside[3] * (PAIR_BASE + PAIR_STEP * beside[4])
        pair_weight = pair_own[..., :, None] * pair_beside[..., None, :]
        weight_pair = cube_slope * (slope_own[..., :, None] * dens_beside[..., None, :] + slope_beside[..., None, :] * dens_own[..., :, None]) + quart_slope * pair_weight
        energy_terms = quart * pair_weight
        if offset == (0, 0, 0):
            weight_pair = weight_pair * self_mask
            energy_terms = energy_terms * self_mask
        total = total + 2.0 * jnp.stack([lax.optimization_barrier(jnp.sum(weight_pair * parts[comp], axis=-1)) for comp in range(3)])
        pair_total = pair_total + lax.optimization_barrier(jnp.sum(energy_terms, axis=-1))
    return (total, pair_total)

def surround(field):
    lead = field.ndim - 4
    wrapped = jnp.pad(field, [(0, 0)] * lead + [(1, 1), (1, 1), (0, 0), (0, 0)], mode='wrap')
    return jnp.pad(wrapped, [(0, 0)] * lead + [(0, 0), (0, 0), (1, 1), (0, 0)])

def reference(positions, species, counts):
    occupied = (lax.broadcasted_iota(jnp.int32, species.shape, 3) < counts[..., None]).astype(jnp.float32)
    state = jnp.concatenate([positions, occupied[None], species.astype(jnp.float32)[None]], axis=0)
    extended = surround(state)
    starts = jnp.arange(NTX, dtype=jnp.int32)

    def density_slab(start):
        return densities(lax.dynamic_slice_in_dim(extended, start, 3, axis=1))[0]
    density = lax.map(density_slab, starts)
    embed, derivative = embedding(density, state)
    derivative_ext = surround(derivative)

    def force_slab(start):
        piece = lax.dynamic_slice_in_dim(extended, start, 3, axis=1)
        slope_piece = lax.dynamic_slice_in_dim(derivative_ext, start, 3, axis=0)
        force_piece, pair_piece = forces_of(piece, slope_piece)
        return (force_piece[:, 0], pair_piece[0])
    force_rows, pair_rows = lax.map(force_slab, starts)
    forces = jnp.moveaxis(force_rows, 1, 0)
    return (forces, embed + 0.5 * pair_rows)
```

```python
import functools

import jax
import jax.numpy as jnp
from jax import lax
from jax.experimental import pallas as pl
from jax.experimental.pallas import tpu as pltpu
from jax.sharding import PartitionSpec as P

CUTOFF_SQUARED = 0.2025
INVERSE_CUTOFF = 1.0 / 0.45
DENSITY_STEP = 0.4
CUBE_ROOT_STEP = 1.4 ** (1.0 / 3.0) - 1.0
EMBED_STEP = -0.3
PAIR_BASE = 0.6
PAIR_STEP = 0.3

F32 = jnp.float32
BF16 = jnp.bfloat16
OCTANTS = [(bx, by, bz) for bx in (0, 1) for by in (0, 1) for bz in (0, 1)]


def rows_iota(shape):
    return lax.broadcasted_iota(jnp.int32, shape, 0)


def lanes_iota(shape):
    return lax.broadcasted_iota(jnp.int32, shape, 1)


def split_three(value):
    first = value.astype(BF16).astype(F32)
    rest = value - first
    second = rest.astype(BF16).astype(F32)
    third = (rest - second).astype(BF16).astype(F32)
    return first, second, third


def left_stack(value):
    one, two, three = split_three(value)
    return jnp.concatenate([one, two, one, two, three, one], axis=0)


def right_stack(value):
    one, two, three = split_three(value)
    return jnp.concatenate([one, one, two, two, one, three], axis=0)


def block_diagonal(first, second):
    depth = first.shape[0]
    zero = jnp.zeros_like(first)
    pad = jnp.zeros((128 - 2 * depth, 256), F32)
    top = jnp.concatenate([first, zero], axis=1)
    low = jnp.concatenate([zero, second], axis=1)
    return jnp.concatenate([top, low, pad], axis=0).astype(BF16)


def row_choice(rows, pairs, other):
    for row, value in pairs:
        other = jnp.where(rows == row, value, other)
    return other


def bits_row(rows, bits):
    return row_choice(rows, [(k, float(b)) for k, b in enumerate(bits) if b], jnp.zeros(rows.shape, F32))


def norm_row(value):
    square = value * value
    return square[0:1] + square[1:2] + square[2:3]


def octant_masks(feature, rows):
    bit = jnp.where(feature >= 0.5, 1, 0)
    octant = 4 * bit[0:1] + 2 * bit[1:2] + bit[2:3]
    octant = jnp.where(feature[3:4] > 0.5, octant, 8)
    return jnp.where(octant == rows, 1.0, 0.0).astype(F32)


def sublane_exclusive(value, rows):
    total = value
    for step in (1, 2, 4):
        total = total + jnp.where(rows >= step, pltpu.roll(total, step, 0), 0.0)
    return total - value


def sort_kernel(state_ref, sorted_ref, rank_ref):
    tiles = state_ref.shape[0]
    rows = rows_iota((8, 128))
    wide_rows = rows_iota((128, 128))
    wide_lanes = lanes_iota((128, 128))
    triangle = jnp.where(wide_rows <= wide_lanes, 1.0, 0.0).astype(BF16)
    lane = lanes_iota((1, 128))
    for tile in range(tiles):
        feature = state_ref[tile]
        mask = octant_masks(feature, rows)
        prefix = jnp.dot(mask.astype(BF16), triangle, preferred_element_type=F32)
        total = jnp.broadcast_to(jnp.sum(mask, axis=1, keepdims=True), (8, 128))
        start = sublane_exclusive(total, rows)
        place = jnp.sum(mask * (prefix - 1.0 + start), axis=0, keepdims=True)
        rank = jnp.where(feature[3:4] > 0.5, place.astype(jnp.int32), lane)
        chosen = jnp.where(jnp.broadcast_to(rank, (128, 128)) == wide_rows, 1.0, 0.0).astype(BF16)
        one, two, three = split_three(feature)
        pieces = jnp.concatenate([one, two, three, jnp.zeros_like(one)], axis=0).astype(BF16)
        moved = lax.dot_general(
            pieces, chosen, (((1,), (1,)), ((), ())), preferred_element_type=F32
        )
        sorted_ref[tile] = (moved[16:24] + moved[8:16]) + moved[0:8]
        rank_ref[tile] = jnp.broadcast_to(rank, (8, 128))


def main_kernel(
    own, ext_ref, rank_ref, force_ref, energy_ref,
    size_ref, start_ref, left_ref, dual_ref, base_ref, density_ref, own_ref, acc_ref, cell_ref, wide_ref, spread_ref,
):
    lx, ly, lz = own
    ny, nz = ly + 2, lz + 2
    tiles = ext_ref.shape[0]
    rows = rows_iota((8, 128))
    lane = lanes_iota((1, 128))

    def tile_of(x, y, z):
        return (x * ny + y) * nz + z

    @pl.loop(0, tiles)
    def _(tile):
        feature = ext_ref[tile]
        mask = octant_masks(feature, rows)
        total = jnp.broadcast_to(jnp.sum(mask, axis=1, keepdims=True), (8, 128))
        size_ref[tile] = total.astype(jnp.int32)
        start_ref[tile] = sublane_exclusive(total, rows).astype(jnp.int32)
        scaled = (feature - 0.5) * INVERSE_CUTOFF
        weight = feature[3:4] * (1.0 + CUBE_ROOT_STEP * feature[4:5])
        left = row_choice(rows, [(3, 1.0), (4, norm_row(scaled))], jnp.where(rows < 3, scaled, 0.0)) * weight
        stack = left_stack(left)
        full = jnp.concatenate([stack, pltpu.roll(stack, 64, 1), jnp.zeros((32, 128), F32)], axis=0)
        left_ref[tile] = full.T[0:64].astype(BF16)

    @pl.loop(0, density_ref.shape[0])
    def _(tile):
        density_ref[tile] = jnp.zeros((8, 128), F32)
        for k in range(4):
            acc_ref[tile, k] = jnp.zeros((8, 128), F32)

    cells = (lx + 1, ly + 1, lz + 1)

    def own_tile(x, y, z):
        inside = (x >= 1) & (x <= lx) & (y >= 1) & (y <= ly) & (z >= 1) & (z <= lz)
        return inside, ((x - 1) * ly + (y - 1)) * lz + (z - 1)

    def cell_tiles(cell):
        a = cell // (cells[1] * cells[2])
        b = (cell // cells[2]) % cells[1]
        c = cell % cells[2]
        return [(a + 1 - bits[0], b + 1 - bits[1], c + 1 - bits[2]) for bits in OCTANTS]

    def density_cell(cell, slot):
        around = cell_tiles(cell)
        base = jnp.zeros((1, 128), jnp.int32)
        for k in range(8):
            base_ref[k : k + 1] = base
            base = base + size_ref[tile_of(*around[k]), k : k + 1]
        count = jnp.max(base)

        def chunk(index, slot):
            cell_ref[slot] = cell
            packed = jnp.zeros((8, 128), F32)
            for k, bits in enumerate(OCTANTS):
                tile = tile_of(*around[k])
                place = lane + 128 * index - base_ref[k : k + 1]
                inside = (place >= 0) & (place < size_ref[tile, k : k + 1])
                source = jnp.broadcast_to((place + start_ref[tile, k : k + 1]) & 127, (8, 128))
                moved = jnp.take_along_axis(ext_ref[tile], source, axis=1)
                packed = jnp.where(jnp.broadcast_to(inside, (8, 128)), moved - bits_row(rows, bits), packed)
            acc = jnp.zeros((8, 256), F32)
            for k, bits in enumerate(OCTANTS):
                tile = tile_of(*around[k])
                scaled = (packed + (bits_row(rows, bits) - 0.5)) * INVERSE_CUTOFF
                right = row_choice(
                    rows, [(3, 1.0 - norm_row(scaled)), (4, -1.0)], jnp.where(rows < 3, 2.0 * scaled, 0.0)
                )
                stack = right_stack(right)
                reach = jnp.dot(left_ref[tile], block_diagonal(stack, stack), preferred_element_type=F32)
                reach = jnp.maximum(reach, 0.0)
                cube = reach * reach * reach
                for part in range(8):
                    acc = acc + cube[8 * part : 8 * part + 8]
            both = acc[:, 0:128] + acc[:, 128:256]
            occupied, species = packed[3:4], packed[4:5]
            weight = occupied * (1.0 + DENSITY_STEP * species)
            density = jnp.sum(both, axis=0, keepdims=True) - weight
            slope = -0.5 * (occupied * (1.0 + EMBED_STEP * species)) / jnp.sqrt(1.0 + density)
            pair = occupied * (PAIR_BASE + PAIR_STEP * species)
            dual_ref[slot] = row_choice(rows, [(3, weight), (4, pair), (5, slope)], packed)
            wide_density = jnp.broadcast_to(density, (8, 128))
            for k, bits in enumerate(OCTANTS):
                inside, mine = own_tile(*around[k])

                @pl.when(inside)
                def _():
                    tile = tile_of(*around[k])
                    local = lane - start_ref[tile, k : k + 1]
                    place = local + base_ref[k : k + 1] - 128 * index
                    keep = (local >= 0) & (local < size_ref[tile, k : k + 1]) & (place >= 0) & (place < 128)
                    moved = jnp.take_along_axis(wide_density, jnp.broadcast_to(place & 127, (8, 128)), axis=1)
                    density_ref[mine] = jnp.where(jnp.broadcast_to(keep, (8, 128)), moved, density_ref[mine])

            return slot + 1

        return lax.fori_loop(0, (count + 127) // 128, chunk, slot)

    slots = lax.fori_loop(0, cells[0] * cells[1] * cells[2], density_cell, jnp.int32(0))

    for x in range(lx):
        for y in range(ly):
            for z in range(lz):
                mine = (x * ly + y) * lz + z
                feature = ext_ref[tile_of(x + 1, y + 1, z + 1)]
                occupied, species = feature[3:4], feature[4:5]
                strength = occupied * (1.0 + EMBED_STEP * species)
                root = jnp.sqrt(1.0 + density_ref[mine][0:1])
                own_ref[mine] = row_choice(
                    rows,
                    [
                        (3, occupied * (1.0 + DENSITY_STEP * species)),
                        (4, occupied * (PAIR_BASE + PAIR_STEP * species)),
                        (5, -0.5 * strength / root),
                        (6, -strength * root),
                    ],
                    feature,
                )

    @pl.loop(0, slots)
    def _(slot):
        around = cell_tiles(cell_ref[slot])
        packed = dual_ref[slot]
        scaled = packed * INVERSE_CUTOFF
        pair = packed[4:5]
        left = row_choice(rows, [(3, 1.0), (4, norm_row(scaled))], jnp.where(rows < 3, scaled, 0.0))
        other = row_choice(rows, [(5, packed[3:4]), (6, packed[5:6])], left * pair)
        full = jnp.concatenate(
            [left_stack(left), left_stack(other), packed, jnp.zeros((24, 128), F32)], axis=0
        ).T
        wide_ref[...] = full.astype(BF16)
        for k, column in enumerate((96, 97, 98, 100)):
            spread_ref[k] = jnp.broadcast_to(full[:, column : column + 1], (128, 128))
        for k, bits in enumerate(OCTANTS):
            inside, mine = own_tile(*around[k])

            @pl.when(inside)
            def _():
                feature = own_ref[mine]
                moved = feature - bits_row(rows, bits)
                scaled = moved * INVERSE_CUTOFF
                right = row_choice(
                    rows, [(3, 1.0 - norm_row(scaled)), (4, -1.0)], jnp.where(rows < 3, 2.0 * scaled, 0.0)
                )
                mixed = row_choice(
                    rows, [(5, feature[5:6]), (6, feature[3:4])], right * ((4.0 / 3.0) * feature[4:5])
                )
                both = jnp.dot(
                    wide_ref[...], block_diagonal(right_stack(right), right_stack(mixed)), preferred_element_type=F32
                )
                sums = [jnp.zeros((8, 128), F32) for _ in range(5)]
                for part in range(16):
                    span = slice(8 * part, 8 * part + 8)
                    reach = jnp.maximum(both[span, 0:128], 0.0)
                    square = reach * reach
                    coef = square * both[span, 128:256]
                    for axis in range(3):
                        sums[axis] = sums[axis] + coef * spread_ref[axis, span]
                    sums[3] = sums[3] + square * square * spread_ref[3, span]
                    sums[4] = sums[4] + coef
                for axis in range(3):
                    acc_ref[mine, axis] += sums[axis] - moved[axis : axis + 1] * sums[4]
                acc_ref[mine, 3] += sums[3]

    for x in range(lx):
        for y in range(ly):
            for z in range(lz):
                mine = (x * ly + y) * lz + z
                feature = own_ref[mine]
                parts = [jnp.sum(acc_ref[mine, k], axis=0, keepdims=True) for k in range(4)]
                pair = feature[4:5]
                energy = feature[6:7] + 0.5 * pair * (parts[3] - pair)
                result = row_choice(
                    rows,
                    [(k, parts[k] * (-6.0 / CUTOFF_SQUARED)) for k in range(3)],
                    jnp.broadcast_to(energy, (8, 128)),
                )
                result = jnp.take_along_axis(result, rank_ref[mine], axis=1)
                for axis in range(3):
                    force_ref[axis, x, y, z : z + 1] = result[axis : axis + 1]
                energy_ref[x, y, z : z + 1] = result[3:4]


def extended(block, axis, dim, periodic):
    count = lax.axis_size(axis)
    size = block.shape[dim]
    forward = [(i, i + 1) for i in range(count - 1)]
    if periodic:
        forward.append((count - 1, 0))
    backward = [(target, source) for source, target in forward]
    first = lax.slice_in_dim(block, 0, 1, axis=dim)
    last = lax.slice_in_dim(block, size - 1, size, axis=dim)
    if periodic and count == 2 and size == 2:
        other = lax.ppermute(block, axis, forward)
        low = lax.slice_in_dim(other, 1, 2, axis=dim)
        high = lax.slice_in_dim(other, 0, 1, axis=dim)
    else:
        low = lax.ppermute(last, axis, forward)
        high = lax.ppermute(first, axis, backward)
    return jnp.concatenate([low, block, high], axis=dim)


def shards(positions, species, counts):
    lx, ly, lz, width = species.shape
    own = (lx, ly, lz)
    mine = lx * ly * lz
    occupied = (lax.broadcasted_iota(jnp.int32, species.shape, 3) < counts[..., None]).astype(F32)
    state = jnp.stack(
        [positions[0], positions[1], positions[2], occupied, species.astype(F32)]
        + [jnp.zeros(species.shape, F32)] * 3,
        axis=3,
    )
    vmem = pl.BlockSpec(memory_space=pltpu.VMEM)
    block, rank = pl.pallas_call(
        sort_kernel,
        out_shape=(
            jax.ShapeDtypeStruct((mine, 8, width), F32),
            jax.ShapeDtypeStruct((mine, 8, width), jnp.int32),
        ),
        in_specs=[vmem],
        out_specs=(vmem, vmem),
        name="sort",
    )(state.reshape(mine, 8, width))
    block = block.reshape(lx, ly, lz, 8, width)
    for axis, dim, periodic in (("gx", 0, True), ("gy", 1, True), ("gz", 2, False)):
        block = extended(block, axis, dim, periodic)
    tiles = (lx + 2) * (ly + 2) * (lz + 2)
    cells = (lx + 1) * (ly + 1) * (lz + 1)
    slots = cells + tiles
    return pl.pallas_call(
        functools.partial(main_kernel, own),
        out_shape=(
            jax.ShapeDtypeStruct((3, lx, ly, lz, width), F32),
            jax.ShapeDtypeStruct((lx, ly, lz, width), F32),
        ),
        in_specs=[vmem, vmem],
        out_specs=(vmem, vmem),
        scratch_shapes=[
            pltpu.VMEM((tiles, 8, 128), jnp.int32),
            pltpu.VMEM((tiles, 8, 128), jnp.int32),
            pltpu.VMEM((tiles, 64, 128), BF16),
            pltpu.VMEM((slots, 8, 128), F32),
            pltpu.VMEM((8, 128), jnp.int32),
            pltpu.VMEM((mine, 8, 128), F32),
            pltpu.VMEM((mine, 8, 128), F32),
            pltpu.VMEM((mine, 4, 8, 128), F32),
            pltpu.SMEM((slots,), jnp.int32),
            pltpu.VMEM((128, 128), BF16),
            pltpu.VMEM((4, 128, 128), F32),
        ],
        name="atoms",
    )(block.reshape(tiles, 8, width), rank)


def solution(mesh):
    placed = (P(None, "gx", "gy", "gz", None), P("gx", "gy", "gz", None), P("gx", "gy", "gz"))
    return jax.shard_map(
        shards,
        mesh=mesh,
        in_specs=placed,
        out_specs=(P(None, "gx", "gy", "gz", None), P("gx", "gy", "gz", None)),
        check_vma=False,
    )
```

```python
import functools

import jax
import jax.numpy as jnp
from jax import lax
from jax.experimental import pallas as pl
from jax.experimental.pallas import tpu as pltpu
from jax.sharding import PartitionSpec as P

CUTOFF_SQUARED = 0.2025
INVERSE_CUTOFF = 1.0 / 0.45
DENSITY_STEP = 0.4
CUBE_ROOT_STEP = 1.4 ** (1.0 / 3.0) - 1.0
EMBED_STEP = -0.3
PAIR_BASE = 0.6
PAIR_STEP = 0.3

F32 = jnp.float32
BF16 = jnp.bfloat16
OCTANTS = [(bx, by, bz) for bx in (0, 1) for by in (0, 1) for bz in (0, 1)]


def rows_iota(shape):
    return lax.broadcasted_iota(jnp.int32, shape, 0)


def lanes_iota(shape):
    return lax.broadcasted_iota(jnp.int32, shape, 1)


def split_three(value):
    first = value.astype(BF16).astype(F32)
    rest = value - first
    second = rest.astype(BF16).astype(F32)
    third = (rest - second).astype(BF16).astype(F32)
    return first, second, third


def left_stack(value):
    one, two, three = split_three(value)
    return jnp.concatenate([one, two, one, two, three, one], axis=0)


def right_stack(value):
    one, two, three = split_three(value)
    return jnp.concatenate([one, one, two, two, one, three], axis=0)


def block_diagonal(first, second):
    depth = first.shape[0]
    zero = jnp.zeros_like(first)
    pad = jnp.zeros((128 - 2 * depth, 256), F32)
    top = jnp.concatenate([first, zero], axis=1)
    low = jnp.concatenate([zero, second], axis=1)
    return jnp.concatenate([top, low, pad], axis=0).astype(BF16)


def row_choice(rows, pairs, other):
    for row, value in pairs:
        other = jnp.where(rows == row, value, other)
    return other


def norm_row(value):
    square = value * value
    return square[0:1] + square[1:2] + square[2:3]


def octant_masks(feature, rows):
    bit = jnp.where(feature >= 0.5, 1, 0)
    octant = 4 * bit[0:1] + 2 * bit[1:2] + bit[2:3]
    octant = jnp.where(feature[3:4] > 0.5, octant, 8)
    return jnp.where(octant == rows, 1.0, 0.0).astype(F32)


def sublane_exclusive(value, rows):
    total = value
    for step in (1, 2, 4):
        total = total + jnp.where(rows >= step, pltpu.roll(total, step, 0), 0.0)
    return total - value


def sort_kernel(state_ref, sorted_ref, rank_ref):
    tiles = state_ref.shape[0]
    rows = rows_iota((8, 128))
    wide_rows = rows_iota((128, 128))
    wide_lanes = lanes_iota((128, 128))
    triangle = jnp.where(wide_rows <= wide_lanes, 1.0, 0.0).astype(BF16)
    lane = lanes_iota((1, 128))
    for tile in range(tiles):
        feature = state_ref[tile]
        mask = octant_masks(feature, rows)
        prefix = jnp.dot(mask.astype(BF16), triangle, preferred_element_type=F32)
        total = jnp.broadcast_to(jnp.sum(mask, axis=1, keepdims=True), (8, 128))
        start = sublane_exclusive(total, rows)
        place = jnp.sum(mask * (prefix - 1.0 + start), axis=0, keepdims=True)
        rank = jnp.where(feature[3:4] > 0.5, place.astype(jnp.int32), lane)
        chosen = jnp.where(jnp.broadcast_to(rank, (128, 128)) == wide_rows, 1.0, 0.0).astype(BF16)
        one, two, three = split_three(feature)
        pieces = jnp.concatenate([one, two, three, jnp.zeros_like(one)], axis=0).astype(BF16)
        moved = lax.dot_general(
            pieces, chosen, (((1,), (1,)), ((), ())), preferred_element_type=F32
        )
        sorted_ref[tile] = (moved[16:24] + moved[8:16]) + moved[0:8]
        rank_ref[tile] = jnp.broadcast_to(rank, (8, 128))


def main_kernel(
    own, ext_ref, rank_ref, force_ref, energy_ref,
    frame_ref, size_ref, start_ref, left_ref, cell_ref, base_ref, dense_ref, dual_ref, count_ref, mine_ref,
    own_ref, acc_ref, pick_ref, wide_ref, spread_ref, table_ref, extra_cell_ref, extra_index_ref, copied,
):
    lx, ly, lz = own
    nx, ny, nz = lx + 2, ly + 2, lz + 2
    cx, cy, cz = lx + 1, ly + 1, lz + 1
    rows = rows_iota((8, 128))
    lane = lanes_iota((8, 128))
    zero = jnp.zeros((8, 128), F32)

    def tile_of(x, y, z):
        return (x * ny + y) * nz + z

    def cell_of(a, b, c):
        return (a * cy + b) * cz + c

    def mine_of(x, y, z):
        return ((x - 1) * ly + (y - 1)) * lz + (z - 1)

    def along(value, source):
        return jnp.take_along_axis(value, source, axis=1, mode="promise_in_bounds")

    def spread_row(ref, index, row):
        return jnp.broadcast_to(ref[index, row : row + 1], (8, 128))

    def right_rows(scaled):
        return row_choice(
            rows, [(3, 1.0 - norm_row(scaled)), (4, -1.0)], jnp.where(rows < 3, 2.0 * scaled, 0.0)
        )

    pick_rows = rows_iota((128, 512))
    pick_group = lanes_iota((128, 512)) // 128
    first_row = jnp.where(pick_group == 3, 51, pick_group)
    chosen = (pick_rows == first_row) | (pick_rows == first_row + 8) | (pick_rows == first_row + 32)
    pick_ref[...] = jnp.where(chosen, 1.0, 0.0).astype(BF16)

    @pl.loop(0, nx * ny)
    def _(column):
        middle = jnp.where(
            rows == 0,
            (column // ny).astype(F32) - 0.5 * nx,
            (column % ny).astype(F32) - 0.5 * ny,
        )
        for z in range(nz):
            tile = column * nz + z
            feature = ext_ref[tile]
            mask = octant_masks(feature, rows)
            total = jnp.broadcast_to(jnp.sum(mask, axis=1, keepdims=True), (8, 128))
            size_ref[tile] = total.astype(jnp.int32)
            start_ref[tile] = sublane_exclusive(total, rows).astype(jnp.int32)
            scaled = (feature + jnp.where(rows == 2, z - 0.5 * nz, middle)) * INVERSE_CUTOFF
            frame_ref[tile] = jnp.where(rows < 3, scaled, feature)
            weight = feature[3:4] * (1.0 + CUBE_ROOT_STEP * feature[4:5])
            left = row_choice(rows, [(3, 1.0), (4, norm_row(scaled))], jnp.where(rows < 3, scaled, 0.0)) * weight
            stack = left_stack(left)
            full = jnp.concatenate([stack, pltpu.roll(stack, 64, 1), jnp.zeros((32, 128), F32)], axis=0)
            left_ref[tile] = full.T[0:64].astype(BF16)

    @pl.loop(0, cx * cy)
    def _(column):
        a, b = column // cy, column % cy
        for c in range(cz):
            cell = column * cz + c
            base = jnp.zeros((8, 128), jnp.int32)
            packed = zero
            for k, (bx, by, bz) in enumerate(OCTANTS):
                tile = tile_of(a + 1 - bx, b + 1 - by, c + 1 - bz)
                base_ref[cell, k] = base
                moved = along(frame_ref[tile], (lane + (spread_row(start_ref, tile, k) - base)) & 127)
                packed = jnp.where(lane >= base, moved, packed)
                base = base + spread_row(size_ref, tile, k)
            cell_ref[cell] = jnp.where(lane < base, packed, 0.0)
            count_ref[pl.ds(cell, 1)] = base[0:1]

    counting = pltpu.make_async_copy(count_ref, table_ref, copied)
    counting.start()
    counting.wait()

    def density_of(packed, tiles):
        stack = right_stack(right_rows(packed))
        right = block_diagonal(stack, stack)
        acc = jnp.zeros((8, 256), F32)
        for tile in tiles:
            reach = jnp.dot(left_ref[tile], right, preferred_element_type=F32)
            reach = jnp.maximum(reach, 0.0)
            cube = reach * reach * reach
            for part in range(8):
                acc = acc + cube[8 * part : 8 * part + 8]
        both = acc[:, 0:128] + acc[:, 128:256]
        occupied, species = packed[3:4], packed[4:5]
        weight = occupied * (1.0 + DENSITY_STEP * species)
        density = jnp.sum(both, axis=0, keepdims=True) - weight
        slope = -0.5 * (occupied * (1.0 + EMBED_STEP * species)) / jnp.sqrt(1.0 + density)
        pair = occupied * (PAIR_BASE + PAIR_STEP * species)
        dual = row_choice(rows, [(3, weight), (4, pair), (5, slope)], packed)
        return jnp.broadcast_to(density, (8, 128)), dual

    def density_column(column, extras):
        a, b = column // cy, column % cy
        for c in range(cz):
            cell = column * cz + c
            tiles = [tile_of(a + 1 - bx, b + 1 - by, c + 1 - bz) for bx, by, bz in OCTANTS]
            dense_ref[cell], dual_ref[cell] = density_of(cell_ref[cell], tiles)
            count = table_ref[cell, 0]

            def put(index, extras):
                extra_cell_ref[extras] = cell
                extra_index_ref[extras] = index
                return extras + 1

            extras = lax.fori_loop(1, (count + 127) // 128, put, extras)
        return extras

    extras = lax.fori_loop(0, cx * cy, density_column, jnp.int32(0))

    @pl.loop(0, lx * ly)
    def _(column):
        x, y = column // ly + 1, column % ly + 1
        for z in range(1, lz + 1):
            tile = tile_of(x, y, z)
            density = zero
            for k, (bx, by, bz) in enumerate(OCTANTS):
                cell = cell_of(x + bx - 1, y + by - 1, z + bz - 1)
                start = spread_row(start_ref, tile, k)
                moved = along(dense_ref[cell], (lane + (base_ref[cell, k] - start)) & 127)
                density = jnp.where(lane >= start, moved, density)
            mine_ref[column * lz + z - 1] = density

    def around(cell):
        a = cell // (cy * cz)
        b = (cell // cz) % cy
        c = cell % cz
        return [(a + 1 - bx, b + 1 - by, c + 1 - bz) for bx, by, bz in OCTANTS]

    def own_tile(x, y, z):
        inside = (x >= 1) & (x <= lx) & (y >= 1) & (y <= ly) & (z >= 1) & (z <= lz)
        return inside, mine_of(x, y, z)

    @pl.loop(0, extras)
    def _(extra):
        cell, index = extra_cell_ref[extra], extra_index_ref[extra]
        near = around(cell)
        tiles = [tile_of(*place) for place in near]
        packed = zero
        for k, tile in enumerate(tiles):
            place = lane + 128 * index - base_ref[cell, k]
            inside = (place >= 0) & (place < spread_row(size_ref, tile, k))
            moved = along(frame_ref[tile], (place + spread_row(start_ref, tile, k)) & 127)
            packed = jnp.where(inside, moved, packed)
        density, dual_ref[cx * cy * cz + extra] = density_of(packed, tiles)
        for k, tile in enumerate(tiles):
            inside, mine = own_tile(*near[k])

            @pl.when(inside)
            def _():
                local = lane - spread_row(start_ref, tile, k)
                place = local + base_ref[cell, k] - 128 * index
                keep = (local >= 0) & (local < spread_row(size_ref, tile, k)) & (place >= 0) & (place < 128)
                mine_ref[mine] = jnp.where(keep, along(density, place & 127), mine_ref[mine])

    def force_left(packed):
        pair = packed[4:5]
        left = row_choice(rows, [(3, 1.0), (4, norm_row(packed))], jnp.where(rows < 3, packed, 0.0))
        other = row_choice(rows, [(5, packed[3:4]), (6, packed[5:6])], left * pair)
        full = jnp.concatenate([left_stack(left), left_stack(other), jnp.zeros((32, 128), F32)], axis=0)
        wide = full.T.astype(BF16)
        return wide, jnp.dot(wide, pick_ref[...], preferred_element_type=F32)

    def force_right(feature):
        right = right_rows(feature)
        mixed = row_choice(
            rows, [(5, feature[5:6]), (6, feature[3:4])], right * ((4.0 / 3.0) * feature[4:5])
        )
        return block_diagonal(right_stack(right), right_stack(mixed))

    def force_sums(slot, right, sums):
        sums = list(sums)
        both = jnp.dot(wide_ref[slot], right, preferred_element_type=F32)
        for part in range(16):
            span = slice(8 * part, 8 * part + 8)
            reach = jnp.maximum(both[span, 0:128], 0.0)
            square = reach * reach
            coef = square * both[span, 128:256]
            for axis in range(3):
                sums[axis] = sums[axis] + coef * spread_ref[slot, span, 128 * axis : 128 * axis + 128]
            sums[3] = sums[3] + square * square * spread_ref[slot, span, 384:512]
            sums[4] = sums[4] + coef
        return sums

    @pl.loop(0, cx * cy)
    def _(column):
        for c in range(cz):
            cell = column * cz + c
            wide_ref[cell], spread_ref[cell] = force_left(dual_ref[cell])

    @pl.loop(0, lx * ly)
    def _(column):
        x, y = column // ly + 1, column % ly + 1
        for z in range(1, lz + 1):
            mine = column * lz + z - 1
            feature = frame_ref[tile_of(x, y, z)]
            occupied, species = feature[3:4], feature[4:5]
            strength = occupied * (1.0 + EMBED_STEP * species)
            root = jnp.sqrt(1.0 + mine_ref[mine][0:1])
            feature = row_choice(
                rows,
                [
                    (3, occupied * (1.0 + DENSITY_STEP * species)),
                    (4, occupied * (PAIR_BASE + PAIR_STEP * species)),
                    (5, -0.5 * strength / root),
                    (6, -strength * root),
                ],
                feature,
            )
            own_ref[mine] = feature
            right = force_right(feature)
            sums = [zero] * 5
            for bx, by, bz in OCTANTS:
                sums = force_sums(cell_of(x + bx - 1, y + by - 1, z + bz - 1), right, sums)
            for k in range(5):
                acc_ref[mine, k] = sums[k]

    @pl.loop(0, extras)
    def _(extra):
        near = around(extra_cell_ref[extra])
        slot = cx * cy * cz
        wide_ref[slot], spread_ref[slot] = force_left(dual_ref[slot + extra])
        for place in near:
            inside, mine = own_tile(*place)

            @pl.when(inside)
            def _():
                sums = force_sums(slot, force_right(own_ref[mine]), [acc_ref[mine, k] for k in range(5)])
                for k in range(5):
                    acc_ref[mine, k] = sums[k]

    for x in range(lx):
        for y in range(ly):
            for z in range(lz):
                mine = (x * ly + y) * lz + z
                feature = own_ref[mine]
                parts = [jnp.sum(acc_ref[mine, k], axis=0, keepdims=True) for k in range(5)]
                pair = feature[4:5]
                energy = feature[6:7] + 0.5 * pair * (parts[3] - pair)
                scale = -6.0 / (CUTOFF_SQUARED * INVERSE_CUTOFF)
                result = row_choice(
                    rows,
                    [(k, (parts[k] - feature[k : k + 1] * parts[4]) * scale) for k in range(3)],
                    jnp.broadcast_to(energy, (8, 128)),
                )
                result = along(result, rank_ref[mine])
                for axis in range(3):
                    force_ref[axis, x, y, z : z + 1] = result[axis : axis + 1]
                energy_ref[x, y, z : z + 1] = result[3:4]


def extended(block, axis, dim, periodic):
    count = lax.axis_size(axis)
    size = block.shape[dim]
    forward = [(i, i + 1) for i in range(count - 1)]
    if periodic:
        forward.append((count - 1, 0))
    backward = [(target, source) for source, target in forward]
    first = lax.slice_in_dim(block, 0, 1, axis=dim)
    last = lax.slice_in_dim(block, size - 1, size, axis=dim)
    if periodic and count == 2 and size == 2:
        other = lax.ppermute(block, axis, forward)
        low = lax.slice_in_dim(other, 1, 2, axis=dim)
        high = lax.slice_in_dim(other, 0, 1, axis=dim)
    else:
        low = lax.ppermute(last, axis, forward)
        high = lax.ppermute(first, axis, backward)
    return jnp.concatenate([low, block, high], axis=dim)


def shards(positions, species, counts):
    lx, ly, lz, width = species.shape
    own = (lx, ly, lz)
    mine = lx * ly * lz
    occupied = (lax.broadcasted_iota(jnp.int32, species.shape, 3) < counts[..., None]).astype(F32)
    state = jnp.stack(
        [positions[0], positions[1], positions[2], occupied, species.astype(F32)]
        + [jnp.zeros(species.shape, F32)] * 3,
        axis=3,
    )
    vmem = pl.BlockSpec(memory_space=pltpu.VMEM)
    block, rank = pl.pallas_call(
        sort_kernel,
        out_shape=(
            jax.ShapeDtypeStruct((mine, 8, width), F32),
            jax.ShapeDtypeStruct((mine, 8, width), jnp.int32),
        ),
        in_specs=[vmem],
        out_specs=(vmem, vmem),
        name="sort",
    )(state.reshape(mine, 8, width))
    block = block.reshape(lx, ly, lz, 8, width)
    for axis, dim, periodic in (("gx", 0, True), ("gy", 1, True), ("gz", 2, False)):
        block = extended(block, axis, dim, periodic)
    tiles = (lx + 2) * (ly + 2) * (lz + 2)
    cells = (lx + 1) * (ly + 1) * (lz + 1)
    return pl.pallas_call(
        functools.partial(main_kernel, own),
        out_shape=(
            jax.ShapeDtypeStruct((3, lx, ly, lz, width), F32),
            jax.ShapeDtypeStruct((lx, ly, lz, width), F32),
        ),
        in_specs=[vmem, vmem],
        out_specs=(vmem, vmem),
        scratch_shapes=[
            pltpu.VMEM((tiles, 8, 128), F32),
            pltpu.VMEM((tiles, 8, 128), jnp.int32),
            pltpu.VMEM((tiles, 8, 128), jnp.int32),
            pltpu.VMEM((tiles, 64, 128), BF16),
            pltpu.VMEM((cells, 8, 128), F32),
            pltpu.VMEM((cells, 8, 8, 128), jnp.int32),
            pltpu.VMEM((cells, 8, 128), F32),
            pltpu.VMEM((cells + tiles, 8, 128), F32),
            pltpu.VMEM((cells, 128), jnp.int32),
            pltpu.VMEM((mine, 8, 128), F32),
            pltpu.VMEM((mine, 8, 128), F32),
            pltpu.VMEM((mine, 5, 8, 128), F32),
            pltpu.VMEM((128, 512), BF16),
            pltpu.VMEM((cells + 1, 128, 128), BF16),
            pltpu.VMEM((cells + 1, 128, 512), F32),
            pltpu.SMEM((cells, 128), jnp.int32),
            pltpu.SMEM((tiles,), jnp.int32),
            pltpu.SMEM((tiles,), jnp.int32),
            pltpu.SemaphoreType.DMA,
        ],
        name="atoms",
    )(block.reshape(tiles, 8, width), rank)


def solution(mesh):
    placed = (P(None, "gx", "gy", "gz", None), P("gx", "gy", "gz", None), P("gx", "gy", "gz"))
    return jax.shard_map(
        shards,
        mesh=mesh,
        in_specs=placed,
        out_specs=(P(None, "gx", "gy", "gz", None), P("gx", "gy", "gz", None)),
        check_vma=False,
    )
```

```python
import functools

import jax
import jax.numpy as jnp
from jax import lax
from jax.experimental import pallas as pl
from jax.experimental.pallas import tpu as pltpu
from jax.sharding import PartitionSpec as P

CUTOFF_SQUARED = 0.2025
INVERSE_CUTOFF = 1.0 / 0.45
DENSITY_STEP = 0.4
CUBE_ROOT_STEP = 1.4 ** (1.0 / 3.0) - 1.0
EMBED_STEP = -0.3
PAIR_BASE = 0.6
PAIR_STEP = 0.3

F32 = jnp.float32
BF16 = jnp.bfloat16
OCTANTS = [(bx, by, bz) for bx in (0, 1) for by in (0, 1) for bz in (0, 1)]


def rows_iota(shape):
    return lax.broadcasted_iota(jnp.int32, shape, 0)


def lanes_iota(shape):
    return lax.broadcasted_iota(jnp.int32, shape, 1)


def split_three(value):
    first = value.astype(BF16).astype(F32)
    rest = value - first
    second = rest.astype(BF16).astype(F32)
    third = (rest - second).astype(BF16).astype(F32)
    return first, second, third


def left_stack(value):
    one, two, three = split_three(value)
    return jnp.concatenate([one, two, one, two, three, one], axis=0)


def right_stack(value):
    one, two, three = split_three(value)
    return jnp.concatenate([one, one, two, two, one, three], axis=0)


def block_diagonal(first, second):
    depth = first.shape[0]
    zero = jnp.zeros_like(first)
    pad = jnp.zeros((128 - 2 * depth, 256), F32)
    top = jnp.concatenate([first, zero], axis=1)
    low = jnp.concatenate([zero, second], axis=1)
    return jnp.concatenate([top, low, pad], axis=0).astype(BF16)


def row_choice(rows, pairs, other):
    for row, value in pairs:
        other = jnp.where(rows == row, value, other)
    return other


def norm_row(value):
    square = value * value
    return square[0:1] + square[1:2] + square[2:3]


def octant_masks(feature, rows):
    bit = jnp.where(feature >= 0.5, 1, 0)
    octant = 4 * bit[0:1] + 2 * bit[1:2] + bit[2:3]
    octant = jnp.where(feature[3:4] > 0.5, octant, 8)
    return jnp.where(octant == rows, 1.0, 0.0).astype(F32)


def sublane_exclusive(value, rows):
    total = value
    for step in (1, 2, 4):
        total = total + jnp.where(rows >= step, pltpu.roll(total, step, 0), 0.0)
    return total - value


def sort_kernel(position_ref, species_ref, count_ref, sorted_ref, rank_ref):
    lx, ly, lz, _ = species_ref.shape
    rows = rows_iota((8, 128))
    wide_rows = rows_iota((128, 128))
    wide_lanes = lanes_iota((128, 128))
    triangle = jnp.where(wide_rows <= wide_lanes, 1.0, 0.0).astype(BF16)
    lane = lanes_iota((1, 128))
    for x in range(lx):
        for y in range(ly):
            for z in range(lz):
                occupied = jnp.where(lane < count_ref[x, y, z], 1.0, 0.0)
                feature = row_choice(
                    rows,
                    [(k, position_ref[k, x, y, z : z + 1]) for k in range(3)]
                    + [(3, occupied), (4, species_ref[x, y, z : z + 1].astype(F32))],
                    jnp.zeros((8, 128), F32),
                )
                mask = octant_masks(feature, rows)
                prefix = jnp.dot(mask.astype(BF16), triangle, preferred_element_type=F32)
                total = jnp.broadcast_to(jnp.sum(mask, axis=1, keepdims=True), (8, 128))
                start = sublane_exclusive(total, rows)
                place = jnp.sum(mask * (prefix - 1.0 + start), axis=0, keepdims=True)
                rank = jnp.where(occupied > 0.5, place.astype(jnp.int32), lane)
                chosen = jnp.where(jnp.broadcast_to(rank, (128, 128)) == wide_rows, 1.0, 0.0).astype(BF16)
                one, two, three = split_three(feature)
                pieces = jnp.concatenate([one, two, three, jnp.zeros_like(one)], axis=0).astype(BF16)
                moved = lax.dot_general(
                    pieces, chosen, (((1,), (1,)), ((), ())), preferred_element_type=F32
                )
                sorted_ref[x, y, z] = (moved[16:24] + moved[8:16]) + moved[0:8]
                rank_ref[(x * ly + y) * lz + z] = jnp.broadcast_to(rank, (8, 128))


def main_kernel(
    own, ext_ref, rank_ref, force_ref, energy_ref,
    frame_ref, size_ref, start_ref, left_ref, cell_ref, base_ref, dense_ref, dual_ref, count_ref, mine_ref,
    own_ref, acc_ref, pick_ref, wide_ref, spread_ref, table_ref, extra_cell_ref, extra_index_ref, copied,
):
    lx, ly, lz = own
    nx, ny, nz = lx + 2, ly + 2, lz + 2
    cx, cy, cz = lx + 1, ly + 1, lz + 1
    rows = rows_iota((8, 128))
    lane = lanes_iota((8, 128))
    zero = jnp.zeros((8, 128), F32)

    def tile_of(x, y, z):
        return (x * ny + y) * nz + z

    def cell_of(a, b, c):
        return (a * cy + b) * cz + c

    def mine_of(x, y, z):
        return ((x - 1) * ly + (y - 1)) * lz + (z - 1)

    def along(value, source):
        return jnp.take_along_axis(value, source, axis=1, mode="promise_in_bounds")

    def spread_row(ref, index, row):
        return jnp.broadcast_to(ref[index, row : row + 1], (8, 128))

    def right_rows(scaled):
        return row_choice(
            rows, [(3, 1.0 - norm_row(scaled)), (4, -1.0)], jnp.where(rows < 3, 2.0 * scaled, 0.0)
        )

    pick_rows = rows_iota((128, 512))
    pick_group = lanes_iota((128, 512)) // 128
    first_row = jnp.where(pick_group == 3, 51, pick_group)
    chosen = (pick_rows == first_row) | (pick_rows == first_row + 8) | (pick_rows == first_row + 32)
    pick_ref[...] = jnp.where(chosen, 1.0, 0.0).astype(BF16)

    @pl.loop(0, nx)
    def _(x):
        middle = jnp.where(rows == 0, x.astype(F32) - 0.5 * nx, 0.0)
        for y, z in [(y, z) for y in range(ny) for z in range(nz)]:
            tile = tile_of(x, y, z)
            feature = ext_ref[tile]
            mask = octant_masks(feature, rows)
            total = jnp.broadcast_to(jnp.sum(mask, axis=1, keepdims=True), (8, 128))
            size_ref[tile] = total.astype(jnp.int32)
            start_ref[tile] = sublane_exclusive(total, rows).astype(jnp.int32)
            offset = row_choice(rows, [(1, y - 0.5 * ny), (2, z - 0.5 * nz)], middle)
            scaled = (feature + offset) * INVERSE_CUTOFF
            frame_ref[tile] = jnp.where(rows < 3, scaled, feature)
            weight = feature[3:4] * (1.0 + CUBE_ROOT_STEP * feature[4:5])
            left = row_choice(rows, [(3, 1.0), (4, norm_row(scaled))], jnp.where(rows < 3, scaled, 0.0)) * weight
            stack = left_stack(left)
            full = jnp.concatenate([stack, pltpu.roll(stack, 64, 1), jnp.zeros((32, 128), F32)], axis=0)
            left_ref[tile] = full.T[0:64].astype(BF16)

    @pl.loop(0, cx * cy)
    def _(column):
        a, b = column // cy, column % cy
        for c in range(cz):
            cell = column * cz + c
            base = jnp.zeros((8, 128), jnp.int32)
            packed = zero
            for k, (bx, by, bz) in enumerate(OCTANTS):
                tile = tile_of(a + 1 - bx, b + 1 - by, c + 1 - bz)
                base_ref[cell, k] = base
                moved = along(frame_ref[tile], (lane + (spread_row(start_ref, tile, k) - base)) & 127)
                packed = jnp.where(lane >= base, moved, packed)
                base = base + spread_row(size_ref, tile, k)
            cell_ref[cell] = jnp.where(lane < base, packed, 0.0)
            count_ref[pl.ds(cell, 1)] = base[0:1]

    counting = pltpu.make_async_copy(count_ref, table_ref, copied)
    counting.start()

    def density_of(packed, tiles):
        stack = right_stack(right_rows(packed))
        right = block_diagonal(stack, stack)
        acc = jnp.zeros((8, 256), F32)
        for tile in tiles:
            reach = jnp.dot(left_ref[tile], right, preferred_element_type=F32)
            reach = jnp.maximum(reach, 0.0)
            cube = reach * reach * reach
            for part in range(8):
                acc = acc + cube[8 * part : 8 * part + 8]
        both = acc[:, 0:128] + acc[:, 128:256]
        occupied, species = packed[3:4], packed[4:5]
        weight = occupied * (1.0 + DENSITY_STEP * species)
        density = jnp.sum(both, axis=0, keepdims=True) - weight
        slope = -0.5 * (occupied * (1.0 + EMBED_STEP * species)) / jnp.sqrt(1.0 + density)
        pair = occupied * (PAIR_BASE + PAIR_STEP * species)
        dual = row_choice(rows, [(3, weight), (4, pair), (5, slope)], packed)
        return jnp.broadcast_to(density, (8, 128)), dual

    @pl.loop(0, cx * cy)
    def _(column):
        a, b = column // cy, column % cy
        for c in range(cz):
            cell = column * cz + c
            tiles = [tile_of(a + 1 - bx, b + 1 - by, c + 1 - bz) for bx, by, bz in OCTANTS]
            dense_ref[cell], dual_ref[cell] = density_of(cell_ref[cell], tiles)

    counting.wait()
    extras = jnp.int32(0)
    most = jnp.int32(0)
    for cell in range(cx * cy * cz):
        count = table_ref[cell, 0]
        extra_cell_ref[extras] = cell
        extra_index_ref[extras] = 1
        extras = extras + (count > 128).astype(jnp.int32)
        most = jnp.maximum(most, count)
    for x in range(1, lx + 1):
        for y in range(1, ly + 1):
            for z in range(1, lz + 1):
                tile = tile_of(x, y, z)
                density = zero
                for k, (bx, by, bz) in enumerate(OCTANTS):
                    cell = cell_of(x + bx - 1, y + by - 1, z + bz - 1)
                    start = spread_row(start_ref, tile, k)
                    moved = along(dense_ref[cell], (lane + (base_ref[cell, k] - start)) & 127)
                    density = jnp.where(lane >= start, moved, density)
                mine_ref[mine_of(x, y, z)] = density

    def more(cell, extras):
        def put(index, extras):
            extra_cell_ref[extras] = cell
            extra_index_ref[extras] = index
            return extras + 1

        return lax.fori_loop(2, (table_ref[cell, 0] + 127) // 128, put, extras)

    extras = lax.fori_loop(0, jnp.where(most > 256, cx * cy * cz, 0), more, extras)

    def around(cell):
        a = cell // (cy * cz)
        b = (cell // cz) % cy
        c = cell % cz
        return [(a + 1 - bx, b + 1 - by, c + 1 - bz) for bx, by, bz in OCTANTS]

    def own_tile(x, y, z):
        inside = (x >= 1) & (x <= lx) & (y >= 1) & (y <= ly) & (z >= 1) & (z <= lz)
        return inside, mine_of(x, y, z)

    @pl.loop(0, extras)
    def _(extra):
        cell, index = extra_cell_ref[extra], extra_index_ref[extra]
        near = around(cell)
        tiles = [tile_of(*place) for place in near]
        packed = zero
        for k, tile in enumerate(tiles):
            place = lane + 128 * index - base_ref[cell, k]
            inside = (place >= 0) & (place < spread_row(size_ref, tile, k))
            moved = along(frame_ref[tile], (place + spread_row(start_ref, tile, k)) & 127)
            packed = jnp.where(inside, moved, packed)
        density, dual_ref[cx * cy * cz + extra] = density_of(packed, tiles)
        for k, tile in enumerate(tiles):
            inside, mine = own_tile(*near[k])

            @pl.when(inside)
            def _():
                local = lane - spread_row(start_ref, tile, k)
                place = local + base_ref[cell, k] - 128 * index
                keep = (local >= 0) & (local < spread_row(size_ref, tile, k)) & (place >= 0) & (place < 128)
                mine_ref[mine] = jnp.where(keep, along(density, place & 127), mine_ref[mine])

    def force_left(packed):
        pair = packed[4:5]
        left = row_choice(rows, [(3, 1.0), (4, norm_row(packed))], jnp.where(rows < 3, packed, 0.0))
        other = row_choice(rows, [(5, packed[3:4]), (6, packed[5:6])], left * pair)
        full = jnp.concatenate([left_stack(left), left_stack(other), jnp.zeros((32, 128), F32)], axis=0)
        wide = full.T.astype(BF16)
        return wide, jnp.dot(wide, pick_ref[...], preferred_element_type=F32)

    def force_right(feature):
        right = right_rows(feature)
        mixed = row_choice(
            rows, [(5, feature[5:6]), (6, feature[3:4])], right * ((4.0 / 3.0) * feature[4:5])
        )
        return block_diagonal(right_stack(right), right_stack(mixed))

    def force_sums(slot, right, sums):
        sums = list(sums)
        both = jnp.dot(wide_ref[slot], right, preferred_element_type=F32)
        for part in range(16):
            span = slice(8 * part, 8 * part + 8)
            reach = jnp.maximum(both[span, 0:128], 0.0)
            square = reach * reach
            coef = square * both[span, 128:256]
            for axis in range(3):
                sums[axis] = sums[axis] + coef * spread_ref[slot, span, 128 * axis : 128 * axis + 128]
            sums[3] = sums[3] + square * square * spread_ref[slot, span, 384:512]
            sums[4] = sums[4] + coef
        return sums

    @pl.loop(0, cx * cy)
    def _(column):
        for c in range(cz):
            cell = column * cz + c
            wide_ref[cell], spread_ref[cell] = force_left(dual_ref[cell])

    @pl.loop(0, lx * ly)
    def _(column):
        x, y = column // ly + 1, column % ly + 1
        for z in range(1, lz + 1):
            mine = column * lz + z - 1
            feature = frame_ref[tile_of(x, y, z)]
            occupied, species = feature[3:4], feature[4:5]
            strength = occupied * (1.0 + EMBED_STEP * species)
            root = jnp.sqrt(1.0 + mine_ref[mine][0:1])
            feature = row_choice(
                rows,
                [
                    (3, occupied * (1.0 + DENSITY_STEP * species)),
                    (4, occupied * (PAIR_BASE + PAIR_STEP * species)),
                    (5, -0.5 * strength / root),
                    (6, -strength * root),
                ],
                feature,
            )
            own_ref[mine] = feature
            right = force_right(feature)
            sums = [zero] * 5
            for bx, by, bz in OCTANTS:
                sums = force_sums(cell_of(x + bx - 1, y + by - 1, z + bz - 1), right, sums)
            for k in range(5):
                acc_ref[mine, k] = sums[k]

    @pl.loop(0, extras)
    def _(extra):
        near = around(extra_cell_ref[extra])
        slot = cx * cy * cz
        wide_ref[slot], spread_ref[slot] = force_left(dual_ref[slot + extra])
        for place in near:
            inside, mine = own_tile(*place)

            @pl.when(inside)
            def _():
                sums = force_sums(slot, force_right(own_ref[mine]), [acc_ref[mine, k] for k in range(5)])
                for k in range(5):
                    acc_ref[mine, k] = sums[k]

    for x in range(lx):
        for y in range(ly):
            for z in range(lz):
                mine = (x * ly + y) * lz + z
                feature = own_ref[mine]
                parts = [jnp.sum(acc_ref[mine, k], axis=0, keepdims=True) for k in range(5)]
                pair = feature[4:5]
                energy = feature[6:7] + 0.5 * pair * (parts[3] - pair)
                scale = -6.0 / (CUTOFF_SQUARED * INVERSE_CUTOFF)
                result = row_choice(
                    rows,
                    [(k, (parts[k] - feature[k : k + 1] * parts[4]) * scale) for k in range(3)],
                    jnp.broadcast_to(energy, (8, 128)),
                )
                result = along(result, rank_ref[mine])
                for axis in range(3):
                    force_ref[axis, x, y, z : z + 1] = result[axis : axis + 1]
                energy_ref[x, y, z : z + 1] = result[3:4]


def extended(block, axis, dim, periodic):
    count = lax.axis_size(axis)
    size = block.shape[dim]
    forward = [(i, i + 1) for i in range(count - 1)]
    if periodic:
        forward.append((count - 1, 0))
    backward = [(target, source) for source, target in forward]
    first = lax.slice_in_dim(block, 0, 1, axis=dim)
    last = lax.slice_in_dim(block, size - 1, size, axis=dim)
    if periodic and count == 2 and size == 2:
        other = lax.ppermute(block, axis, forward)
        low = lax.slice_in_dim(other, 1, 2, axis=dim)
        high = lax.slice_in_dim(other, 0, 1, axis=dim)
    else:
        low = lax.ppermute(last, axis, forward)
        high = lax.ppermute(first, axis, backward)
    return jnp.concatenate([low, block, high], axis=dim)


def shards(positions, species, counts):
    lx, ly, lz, width = species.shape
    own = (lx, ly, lz)
    mine = lx * ly * lz
    vmem = pl.BlockSpec(memory_space=pltpu.VMEM)
    block, rank = pl.pallas_call(
        sort_kernel,
        out_shape=(
            jax.ShapeDtypeStruct((lx, ly, lz, 8, width), F32),
            jax.ShapeDtypeStruct((mine, 8, width), jnp.int32),
        ),
        in_specs=[vmem, vmem, pl.BlockSpec(memory_space=pltpu.SMEM)],
        out_specs=(vmem, vmem),
        name="sort",
    )(positions, species, counts)
    for axis, dim, periodic in (("gx", 0, True), ("gy", 1, True), ("gz", 2, False)):
        block = extended(block, axis, dim, periodic)
    tiles = (lx + 2) * (ly + 2) * (lz + 2)
    cells = (lx + 1) * (ly + 1) * (lz + 1)
    return pl.pallas_call(
        functools.partial(main_kernel, own),
        out_shape=(
            jax.ShapeDtypeStruct((3, lx, ly, lz, width), F32),
            jax.ShapeDtypeStruct((lx, ly, lz, width), F32),
        ),
        in_specs=[vmem, vmem],
        out_specs=(vmem, vmem),
        scratch_shapes=[
            pltpu.VMEM((tiles, 8, 128), F32),
            pltpu.VMEM((tiles, 8, 128), jnp.int32),
            pltpu.VMEM((tiles, 8, 128), jnp.int32),
            pltpu.VMEM((tiles, 64, 128), BF16),
            pltpu.VMEM((cells, 8, 128), F32),
            pltpu.VMEM((cells, 8, 8, 128), jnp.int32),
            pltpu.VMEM((cells, 8, 128), F32),
            pltpu.VMEM((cells + tiles, 8, 128), F32),
            pltpu.VMEM((cells, 128), jnp.int32),
            pltpu.VMEM((mine, 8, 128), F32),
            pltpu.VMEM((mine, 8, 128), F32),
            pltpu.VMEM((mine, 5, 8, 128), F32),
            pltpu.VMEM((128, 512), BF16),
            pltpu.VMEM((cells + 1, 128, 128), BF16),
            pltpu.VMEM((cells + 1, 128, 512), F32),
            pltpu.SMEM((cells, 128), jnp.int32),
            pltpu.SMEM((tiles + 1,), jnp.int32),
            pltpu.SMEM((tiles + 1,), jnp.int32),
            pltpu.SemaphoreType.DMA,
        ],
        name="atoms",
    )(block.reshape(tiles, 8, width), rank)


def solution(mesh):
    placed = (P(None, "gx", "gy", "gz", None), P("gx", "gy", "gz", None), P("gx", "gy", "gz"))
    return jax.shard_map(
        shards,
        mesh=mesh,
        in_specs=placed,
        out_specs=(P(None, "gx", "gy", "gz", None), P("gx", "gy", "gz", None)),
        check_vma=False,
    )
```

```python
import functools

import jax
import jax.numpy as jnp
from jax import lax
from jax.experimental import pallas as pl
from jax.experimental.pallas import tpu as pltpu
from jax.sharding import PartitionSpec as P

CUTOFF_SQUARED = 0.2025
INVERSE_CUTOFF = 1.0 / 0.45
DENSITY_STEP = 0.4
CUBE_ROOT_STEP = 1.4 ** (1.0 / 3.0) - 1.0
EMBED_STEP = -0.3
LOWEST_LIMIT = 0.455
HIGHEST_LIMIT = 0.545
PAIR_BASE = 0.6
PAIR_STEP = 0.3

F32 = jnp.float32
BF16 = jnp.bfloat16
OCTANTS = [(bx, by, bz) for bx in (0, 1) for by in (0, 1) for bz in (0, 1)]


def rows_iota(shape):
    return lax.broadcasted_iota(jnp.int32, shape, 0)


def lanes_iota(shape):
    return lax.broadcasted_iota(jnp.int32, shape, 1)


def split_three(value):
    first = value.astype(BF16).astype(F32)
    rest = value - first
    second = rest.astype(BF16).astype(F32)
    third = (rest - second).astype(BF16).astype(F32)
    return first, second, third


def left_stack(value):
    one, two, three = split_three(value)
    return jnp.concatenate([one, two, one, two, three, one], axis=0)


def right_stack(value):
    one, two, three = split_three(value)
    return jnp.concatenate([one, one, two, two, one, three], axis=0)


def block_diagonal(first, second):
    depth = first.shape[0]
    zero = jnp.zeros_like(first)
    pad = jnp.zeros((128 - 2 * depth, 256), F32)
    top = jnp.concatenate([first, zero], axis=1)
    low = jnp.concatenate([zero, second], axis=1)
    return jnp.concatenate([top, low, pad], axis=0).astype(BF16)


def row_choice(rows, pairs, other):
    for row, value in pairs:
        other = jnp.where(rows == row, value, other)
    return other


def norm_row(value):
    square = value * value
    return square[0:1] + square[1:2] + square[2:3]


def halves(value, group, limits, order):
    below = jnp.sum(jnp.where(value < limits, group, 0.0), axis=1, keepdims=True)
    total = jnp.sum(group, axis=1, keepdims=True)
    score = jnp.abs(2.0 * below - total) * 8.0 + order
    best = jnp.min(score, axis=0, keepdims=True)
    limit = jnp.max(jnp.where(score == best, limits, 0.0), axis=0, keepdims=True)
    return jnp.where(value >= limit, group, 0.0), jnp.where(value >= limit, 0.0, group)


def sublane_exclusive(value, rows):
    total = value
    for step in (1, 2, 4):
        total = total + jnp.where(rows >= step, pltpu.roll(total, step, 0), 0.0)
    return total - value


def sort_kernel(position_ref, species_ref, count_ref, sorted_ref, rank_ref):
    lx, ly, lz, _ = species_ref.shape
    rows = rows_iota((8, 128))
    wide_rows = rows_iota((128, 128))
    wide_lanes = lanes_iota((128, 128))
    triangle = jnp.where(wide_rows <= wide_lanes, 1.0, 0.0).astype(BF16)
    lane = lanes_iota((1, 128))
    order = rows.astype(F32)
    limits = LOWEST_LIMIT + (HIGHEST_LIMIT - LOWEST_LIMIT) / 7.0 * order
    for x in range(lx):
        for y in range(ly):
            for z in range(lz):
                occupied = jnp.where(lane < count_ref[x, y, z], 1.0, 0.0)
                groups = [jnp.broadcast_to(occupied, (8, 128))]
                for k in range(3):
                    value = jnp.broadcast_to(position_ref[k, x, y, z : z + 1], (8, 128))
                    pairs = [halves(value, group, limits, order) for group in groups]
                    groups = [part for high, low in pairs for part in (low, high)]
                mask = row_choice(rows, list(enumerate(groups))[1:], groups[0])
                octant = jnp.sum(mask * order, axis=0, keepdims=True)
                feature = row_choice(
                    rows,
                    [(k, position_ref[k, x, y, z : z + 1]) for k in range(3)]
                    + [(3, occupied), (4, species_ref[x, y, z : z + 1].astype(F32)), (5, octant)],
                    jnp.zeros((8, 128), F32),
                )
                prefix = jnp.dot(mask.astype(BF16), triangle, preferred_element_type=F32)
                total = jnp.broadcast_to(jnp.sum(mask, axis=1, keepdims=True), (8, 128))
                start = sublane_exclusive(total, rows)
                place = jnp.sum(mask * (prefix - 1.0 + start), axis=0, keepdims=True)
                rank = jnp.where(occupied > 0.5, place.astype(jnp.int32), lane)
                chosen = jnp.where(jnp.broadcast_to(rank, (128, 128)) == wide_rows, 1.0, 0.0).astype(BF16)
                one, two, three = split_three(feature)
                pieces = jnp.concatenate([one, two, three, jnp.zeros_like(one)], axis=0).astype(BF16)
                moved = lax.dot_general(
                    pieces, chosen, (((1,), (1,)), ((), ())), preferred_element_type=F32
                )
                sorted_ref[x, y, z] = ((moved[16:24] + moved[8:16]) + moved[0:8])[0:6]
                rank_ref[(x * ly + y) * lz + z] = jnp.broadcast_to(rank, (8, 128))


def main_kernel(
    own, ext_ref, rank_ref, force_ref, energy_ref,
    frame_ref, size_ref, start_ref, left_ref, cell_ref, base_ref, dense_ref, dual_ref, count_ref, mine_ref,
    own_ref, acc_ref, pick_ref, wide_ref, spread_ref, table_ref, extra_cell_ref, extra_index_ref, copied,
):
    lx, ly, lz = own
    nx, ny, nz = lx + 2, ly + 2, lz + 2
    cx, cy, cz = lx + 1, ly + 1, lz + 1
    rows = rows_iota((8, 128))
    lane = lanes_iota((8, 128))
    zero = jnp.zeros((8, 128), F32)

    def tile_of(x, y, z):
        return (x * ny + y) * nz + z

    def cell_of(a, b, c):
        return (a * cy + b) * cz + c

    def mine_of(x, y, z):
        return ((x - 1) * ly + (y - 1)) * lz + (z - 1)

    def along(value, source):
        return jnp.take_along_axis(value, source, axis=1, mode="promise_in_bounds")

    def spread_row(ref, index, row):
        return jnp.broadcast_to(ref[index, row : row + 1], (8, 128))

    def right_rows(scaled):
        return row_choice(
            rows, [(3, 1.0 - norm_row(scaled)), (4, -1.0)], jnp.where(rows < 3, 2.0 * scaled, 0.0)
        )

    pick_rows = rows_iota((128, 512))
    pick_group = lanes_iota((128, 512)) // 128
    first_row = jnp.where(pick_group == 3, 51, pick_group)
    chosen = (pick_rows == first_row) | (pick_rows == first_row + 8) | (pick_rows == first_row + 32)
    pick_ref[...] = jnp.where(chosen, 1.0, 0.0).astype(BF16)

    @pl.loop(0, nx)
    def _(x):
        middle = jnp.where(rows == 0, x.astype(F32) - 0.5 * nx, 0.0)
        for y, z in [(y, z) for y in range(ny) for z in range(nz)]:
            tile = tile_of(x, y, z)
            feature = jnp.concatenate([ext_ref[tile], jnp.zeros((2, 128), F32)], axis=0)
            mask = jnp.where(feature[5:6] == rows.astype(F32), feature[3:4], 0.0)
            total = jnp.broadcast_to(jnp.sum(mask, axis=1, keepdims=True), (8, 128))
            size_ref[tile] = total.astype(jnp.int32)
            start_ref[tile] = sublane_exclusive(total, rows).astype(jnp.int32)
            offset = row_choice(rows, [(1, y - 0.5 * ny), (2, z - 0.5 * nz)], middle)
            scaled = (feature + offset) * INVERSE_CUTOFF
            frame_ref[tile] = jnp.where(rows < 3, scaled, feature)
            weight = feature[3:4] * (1.0 + CUBE_ROOT_STEP * feature[4:5])
            left = row_choice(rows, [(3, 1.0), (4, norm_row(scaled))], jnp.where(rows < 3, scaled, 0.0)) * weight
            stack = left_stack(left)
            full = jnp.concatenate([stack, pltpu.roll(stack, 64, 1), jnp.zeros((32, 128), F32)], axis=0)
            left_ref[tile] = full.astype(BF16).T[0:64]

    @pl.loop(0, cx)
    def _(a):
        for b, c in [(b, c) for b in range(cy) for c in range(cz)]:
            cell = cell_of(a, b, c)
            base = jnp.zeros((8, 128), jnp.int32)
            packed = zero
            for k, (bx, by, bz) in enumerate(OCTANTS):
                tile = tile_of(a + 1 - bx, b + 1 - by, c + 1 - bz)
                base_ref[cell, k] = base
                moved = along(frame_ref[tile], (lane + (spread_row(start_ref, tile, k) - base)) & 127)
                packed = jnp.where(lane >= base, moved, packed)
                base = base + spread_row(size_ref, tile, k)
            cell_ref[cell] = jnp.where(lane < base, packed, 0.0)
            count_ref[pl.ds(cell, 1)] = base[0:1]

    counting = pltpu.make_async_copy(count_ref, table_ref, copied)
    counting.start()

    def density_of(packed, tiles):
        stack = right_stack(right_rows(packed))
        right = block_diagonal(stack, stack)
        left = jnp.concatenate([left_ref[tile] for tile in tiles], axis=0)
        reach = jnp.maximum(jnp.dot(left, right, preferred_element_type=F32), 0.0)
        cube = reach * reach * reach
        acc = cube[0:8]
        for part in range(1, cube.shape[0] // 8):
            acc = acc + cube[8 * part : 8 * part + 8]
        both = acc[:, 0:128] + acc[:, 128:256]
        occupied, species = packed[3:4], packed[4:5]
        weight = occupied * (1.0 + DENSITY_STEP * species)
        density = jnp.sum(both, axis=0, keepdims=True) - weight
        slope = -0.5 * (occupied * (1.0 + EMBED_STEP * species)) / jnp.sqrt(1.0 + density)
        pair = occupied * (PAIR_BASE + PAIR_STEP * species)
        dual = row_choice(rows, [(3, weight), (4, pair), (5, slope)], packed)
        return jnp.broadcast_to(density, (8, 128)), dual

    @pl.loop(0, cx)
    def _(a):
        for b, c in [(b, c) for b in range(cy) for c in range(cz)]:
            cell = cell_of(a, b, c)
            tiles = [tile_of(a + 1 - bx, b + 1 - by, c + 1 - bz) for bx, by, bz in OCTANTS]
            dense_ref[cell], dual_ref[cell] = density_of(cell_ref[cell], tiles)

    counting.wait()
    extras = jnp.int32(0)
    most = jnp.int32(0)
    for cell in range(cx * cy * cz):
        count = table_ref[cell, 0]
        extra_cell_ref[extras] = cell
        extra_index_ref[extras] = 1
        extras = extras + (count > 128).astype(jnp.int32)
        most = jnp.maximum(most, count)
    for x in range(1, lx + 1):
        for y in range(1, ly + 1):
            for z in range(1, lz + 1):
                tile = tile_of(x, y, z)
                density = zero
                for k, (bx, by, bz) in enumerate(OCTANTS):
                    cell = cell_of(x + bx - 1, y + by - 1, z + bz - 1)
                    start = spread_row(start_ref, tile, k)
                    moved = along(dense_ref[cell], (lane + (base_ref[cell, k] - start)) & 127)
                    density = jnp.where(lane >= start, moved, density)
                mine_ref[mine_of(x, y, z)] = density

    def more(cell, extras):
        def put(index, extras):
            extra_cell_ref[extras] = cell
            extra_index_ref[extras] = index
            return extras + 1

        return lax.fori_loop(2, (table_ref[cell, 0] + 127) // 128, put, extras)

    extras = lax.fori_loop(0, jnp.where(most > 256, cx * cy * cz, 0), more, extras)

    def around(cell):
        a = cell // (cy * cz)
        b = (cell // cz) % cy
        c = cell % cz
        return [(a + 1 - bx, b + 1 - by, c + 1 - bz) for bx, by, bz in OCTANTS]

    def own_tile(x, y, z):
        inside = (x >= 1) & (x <= lx) & (y >= 1) & (y <= ly) & (z >= 1) & (z <= lz)
        return inside, mine_of(x, y, z)

    @pl.loop(0, extras)
    def _(extra):
        cell, index = extra_cell_ref[extra], extra_index_ref[extra]
        near = around(cell)
        tiles = [tile_of(*place) for place in near]
        packed = zero
        for k, tile in enumerate(tiles):
            place = lane + 128 * index - base_ref[cell, k]
            inside = (place >= 0) & (place < spread_row(size_ref, tile, k))
            moved = along(frame_ref[tile], (place + spread_row(start_ref, tile, k)) & 127)
            packed = jnp.where(inside, moved, packed)
        density, dual_ref[cx * cy * cz + extra] = density_of(packed, tiles)
        for k, tile in enumerate(tiles):
            inside, mine = own_tile(*near[k])

            @pl.when(inside)
            def _():
                local = lane - spread_row(start_ref, tile, k)
                place = local + base_ref[cell, k] - 128 * index
                keep = (local >= 0) & (local < spread_row(size_ref, tile, k)) & (place >= 0) & (place < 128)
                mine_ref[mine] = jnp.where(keep, along(density, place & 127), mine_ref[mine])

    def force_left(packed):
        pair = packed[4:5]
        left = row_choice(rows, [(3, 1.0), (4, norm_row(packed))], jnp.where(rows < 3, packed, 0.0))
        other = row_choice(rows, [(5, packed[3:4]), (6, packed[5:6])], left * pair)
        full = jnp.concatenate([left_stack(left), left_stack(other), jnp.zeros((32, 128), F32)], axis=0)
        wide = full.astype(BF16).T
        return wide, jnp.dot(wide, pick_ref[...], preferred_element_type=F32)

    def force_right(feature):
        right = right_rows(feature)
        mixed = row_choice(
            rows, [(5, feature[5:6]), (6, feature[3:4])], right * ((4.0 / 3.0) * feature[4:5])
        )
        return block_diagonal(right_stack(right), right_stack(mixed))

    def force_sums(slots, right, sums):
        sums = list(sums)
        left = jnp.concatenate([wide_ref[slot] for slot in slots], axis=0)
        both = jnp.dot(left, right, preferred_element_type=F32)
        for k, slot in enumerate(slots):
            for part in range(16):
                span = slice(8 * part, 8 * part + 8)
                whole = slice(128 * k + 8 * part, 128 * k + 8 * part + 8)
                reach = jnp.maximum(both[whole, 0:128], 0.0)
                square = reach * reach
                coef = square * both[whole, 128:256]
                for axis in range(3):
                    sums[axis] = sums[axis] + coef * spread_ref[slot, span, 128 * axis : 128 * axis + 128]
                sums[3] = sums[3] + square * square * spread_ref[slot, span, 384:512]
                sums[4] = sums[4] + coef
        return sums

    @pl.loop(0, cx)
    def _(a):
        for plane in range(cy * cz):
            cell = a * (cy * cz) + plane
            wide_ref[cell], spread_ref[cell] = force_left(dual_ref[cell])

    @pl.loop(0, lx * ly)
    def _(column):
        x, y = column // ly + 1, column % ly + 1
        for z in range(1, lz + 1):
            mine = column * lz + z - 1
            feature = frame_ref[tile_of(x, y, z)]
            occupied, species = feature[3:4], feature[4:5]
            strength = occupied * (1.0 + EMBED_STEP * species)
            root = jnp.sqrt(1.0 + mine_ref[mine][0:1])
            feature = row_choice(
                rows,
                [
                    (3, occupied * (1.0 + DENSITY_STEP * species)),
                    (4, occupied * (PAIR_BASE + PAIR_STEP * species)),
                    (5, -0.5 * strength / root),
                    (6, -strength * root),
                ],
                feature,
            )
            own_ref[mine] = feature
            right = force_right(feature)
            slots = [cell_of(x + bx - 1, y + by - 1, z + bz - 1) for bx, by, bz in OCTANTS]
            for k, value in enumerate(force_sums(slots, right, [zero] * 5)):
                acc_ref[mine, k] = value

    @pl.loop(0, extras)
    def _(extra):
        near = around(extra_cell_ref[extra])
        slot = cx * cy * cz
        wide_ref[slot], spread_ref[slot] = force_left(dual_ref[slot + extra])
        for place in near:
            inside, mine = own_tile(*place)

            @pl.when(inside)
            def _():
                sums = force_sums([slot], force_right(own_ref[mine]), [acc_ref[mine, k] for k in range(5)])
                for k in range(5):
                    acc_ref[mine, k] = sums[k]

    for x in range(lx):
        for y in range(ly):
            for z in range(lz):
                mine = (x * ly + y) * lz + z
                feature = own_ref[mine]
                parts = [jnp.sum(acc_ref[mine, k], axis=0, keepdims=True) for k in range(5)]
                pair = feature[4:5]
                energy = feature[6:7] + 0.5 * pair * (parts[3] - pair)
                scale = -6.0 / (CUTOFF_SQUARED * INVERSE_CUTOFF)
                result = row_choice(
                    rows,
                    [(k, (parts[k] - feature[k : k + 1] * parts[4]) * scale) for k in range(3)],
                    jnp.broadcast_to(energy, (8, 128)),
                )
                result = along(result, rank_ref[mine])
                for axis in range(3):
                    force_ref[axis, x, y, z : z + 1] = result[axis : axis + 1]
                energy_ref[x, y, z : z + 1] = result[3:4]


def extended(block, axis, dim, periodic):
    count = lax.axis_size(axis)
    size = block.shape[dim]
    first = lax.slice_in_dim(block, 0, 1, axis=dim)
    last = lax.slice_in_dim(block, size - 1, size, axis=dim)
    if periodic and count == 2 and size == 2:
        other = lax.ppermute(block, axis, [(0, 1), (1, 0)])
        low = lax.slice_in_dim(other, 1, 2, axis=dim)
        high = lax.slice_in_dim(other, 0, 1, axis=dim)
    elif count % 2 == 0:
        place = lax.axis_index(axis)
        even = place % 2 == 0
        inner = [(i, i ^ 1) for i in range(count)]
        outer = [(i, (i - 1 if i % 2 == 0 else i + 1) % count) for i in range(count)]
        if not periodic:
            outer[0], outer[-1] = (0, 0), (count - 1, count - 1)
        near = lax.ppermute(jnp.where(even, last, first), axis, inner)
        far = lax.ppermute(jnp.where(even, first, last), axis, outer)
        if not periodic:
            far = jnp.where((place == 0) | (place == count - 1), 0.0, far)
        low, high = jnp.where(even, far, near), jnp.where(even, near, far)
    else:
        forward = [(i, i + 1) for i in range(count - 1)]
        if periodic:
            forward.append((count - 1, 0))
        backward = [(target, source) for source, target in forward]
        low = lax.ppermute(last, axis, forward)
        high = lax.ppermute(first, axis, backward)
    return jnp.concatenate([low, block, high], axis=dim)


def shards(positions, species, counts):
    lx, ly, lz, width = species.shape
    own = (lx, ly, lz)
    mine = lx * ly * lz
    vmem = pl.BlockSpec(memory_space=pltpu.VMEM)
    block, rank = pl.pallas_call(
        sort_kernel,
        out_shape=(
            jax.ShapeDtypeStruct((lx, ly, lz, 6, width), F32),
            jax.ShapeDtypeStruct((mine, 8, width), jnp.int32),
        ),
        in_specs=[vmem, vmem, pl.BlockSpec(memory_space=pltpu.SMEM)],
        out_specs=(vmem, vmem),
        name="sort",
    )(positions, species, counts)
    for axis, dim, periodic in (("gx", 0, True), ("gy", 1, True), ("gz", 2, False)):
        block = extended(block, axis, dim, periodic)
    tiles = (lx + 2) * (ly + 2) * (lz + 2)
    cells = (lx + 1) * (ly + 1) * (lz + 1)
    return pl.pallas_call(
        functools.partial(main_kernel, own),
        out_shape=(
            jax.ShapeDtypeStruct((3, lx, ly, lz, width), F32),
            jax.ShapeDtypeStruct((lx, ly, lz, width), F32),
        ),
        in_specs=[vmem, vmem],
        out_specs=(vmem, vmem),
        scratch_shapes=[
            pltpu.VMEM((tiles, 8, 128), F32),
            pltpu.VMEM((tiles, 8, 128), jnp.int32),
            pltpu.VMEM((tiles, 8, 128), jnp.int32),
            pltpu.VMEM((tiles, 64, 128), BF16),
            pltpu.VMEM((cells, 8, 128), F32),
            pltpu.VMEM((cells, 8, 8, 128), jnp.int32),
            pltpu.VMEM((cells, 8, 128), F32),
            pltpu.VMEM((cells + tiles, 8, 128), F32),
            pltpu.VMEM((cells, 128), jnp.int32),
            pltpu.VMEM((mine, 8, 128), F32),
            pltpu.VMEM((mine, 8, 128), F32),
            pltpu.VMEM((mine, 5, 8, 128), F32),
            pltpu.VMEM((128, 512), BF16),
            pltpu.VMEM((cells + 1, 128, 128), BF16),
            pltpu.VMEM((cells + 1, 128, 512), F32),
            pltpu.SMEM((cells, 128), jnp.int32),
            pltpu.SMEM((tiles + 1,), jnp.int32),
            pltpu.SMEM((tiles + 1,), jnp.int32),
            pltpu.SemaphoreType.DMA,
        ],
        name="atoms",
    )(block.reshape(tiles, 6, width), rank)


def solution(mesh):
    placed = (P(None, "gx", "gy", "gz", None), P("gx", "gy", "gz", None), P("gx", "gy", "gz"))
    return jax.shard_map(
        shards,
        mesh=mesh,
        in_specs=placed,
        out_specs=(P(None, "gx", "gy", "gz", None), P("gx", "gy", "gz", None)),
        check_vma=False,
    )
```

```python
import functools

import jax
import jax.numpy as jnp
from jax import lax
from jax.experimental import pallas as pl
from jax.experimental.pallas import tpu as pltpu
from jax.sharding import PartitionSpec as P

CUTOFF_SQUARED = 0.2025
INVERSE_CUTOFF = 1.0 / 0.45
DENSITY_STEP = 0.4
CUBE_ROOT_STEP = 1.4 ** (1.0 / 3.0) - 1.0
EMBED_STEP = -0.3
LOWEST_LIMIT = 0.4505
HIGHEST_LIMIT = 0.5495
POOL = 32
PAIR_BASE = 0.6
PAIR_STEP = 0.3

F32 = jnp.float32
BF16 = jnp.bfloat16
OCTANTS = [(bx, by, bz) for bx in (0, 1) for by in (0, 1) for bz in (0, 1)]


def rows_iota(shape):
    return lax.broadcasted_iota(jnp.int32, shape, 0)


def lanes_iota(shape):
    return lax.broadcasted_iota(jnp.int32, shape, 1)


def split_three(value):
    first = value.astype(BF16).astype(F32)
    rest = value - first
    second = rest.astype(BF16).astype(F32)
    third = (rest - second).astype(BF16).astype(F32)
    return first, second, third


def left_stack(value):
    one, two, three = split_three(value)
    return jnp.concatenate([one, two, one, two, three, one], axis=0)


def right_stack(value):
    one, two, three = split_three(value)
    return jnp.concatenate([one, one, two, two, one, three], axis=0)


def block_diagonal(first, second):
    depth = first.shape[0]
    zero = jnp.zeros_like(first)
    pad = jnp.zeros((128 - 2 * depth, 256), F32)
    top = jnp.concatenate([first, zero], axis=1)
    low = jnp.concatenate([zero, second], axis=1)
    return jnp.concatenate([top, low, pad], axis=0).astype(BF16)


def row_choice(rows, pairs, other):
    for row, value in pairs:
        other = jnp.where(rows == row, value, other)
    return other


def norm_row(value):
    square = value * value
    return square[0:1] + square[1:2] + square[2:3]


def halves(value, group, limits, order):
    below = jnp.sum(jnp.where(value < limits, group, 0.0), axis=1, keepdims=True)
    total = jnp.sum(group, axis=1, keepdims=True)
    score = jnp.abs(2.0 * below - total) * 8.0 + order
    best = jnp.min(score, axis=0, keepdims=True)
    limit = jnp.max(jnp.where(score == best, limits, 0.0), axis=0, keepdims=True)
    return jnp.where(value >= limit, group, 0.0), jnp.where(value >= limit, 0.0, group)


def sublane_exclusive(value, rows):
    total = value
    for step in (1, 2, 4):
        total = total + jnp.where(rows >= step, pltpu.roll(total, step, 0), 0.0)
    return total - value


def sort_kernel(position_ref, species_ref, count_ref, sorted_ref):
    lx, ly, lz, _ = species_ref.shape
    rows = rows_iota((8, 128))
    wide_rows = rows_iota((128, 128))
    wide_lanes = lanes_iota((128, 128))
    triangle = jnp.where(wide_rows <= wide_lanes, 1.0, 0.0).astype(BF16)
    lane = lanes_iota((1, 128))
    order = rows.astype(F32)
    limits = LOWEST_LIMIT + (HIGHEST_LIMIT - LOWEST_LIMIT) / 7.0 * order
    for x in range(lx):
        for y in range(ly):
            for z in range(lz):
                occupied = jnp.where(lane < count_ref[x, y, z], 1.0, 0.0)
                groups = [jnp.broadcast_to(occupied, (8, 128))]
                for k in range(3):
                    value = jnp.broadcast_to(position_ref[k, x, y, z : z + 1], (8, 128))
                    pairs = [halves(value, group, limits, order) for group in groups]
                    groups = [part for high, low in pairs for part in (low, high)]
                mask = row_choice(rows, list(enumerate(groups))[1:], groups[0])
                octant = jnp.sum(mask * order, axis=0, keepdims=True)
                feature = row_choice(
                    rows,
                    [(k, position_ref[k, x, y, z : z + 1]) for k in range(3)]
                    + [(3, occupied), (4, species_ref[x, y, z : z + 1].astype(F32)), (5, octant)],
                    jnp.zeros((8, 128), F32),
                )
                prefix = jnp.dot(mask.astype(BF16), triangle, preferred_element_type=F32)
                total = jnp.broadcast_to(jnp.sum(mask, axis=1, keepdims=True), (8, 128))
                start = sublane_exclusive(total, rows)
                place = jnp.sum(mask * (prefix - 1.0 + start), axis=0, keepdims=True)
                rank = jnp.where(occupied > 0.5, place.astype(jnp.int32), lane)
                chosen = jnp.where(jnp.broadcast_to(rank, (128, 128)) == wide_rows, 1.0, 0.0).astype(BF16)
                one, two, three = split_three(feature)
                pieces = jnp.concatenate([one, two, three, jnp.zeros_like(one)], axis=0).astype(BF16)
                moved = lax.dot_general(
                    pieces, chosen, (((1,), (1,)), ((), ())), preferred_element_type=F32
                )
                whole = (moved[16:24] + moved[8:16]) + moved[0:8]
                sorted_ref[x, y, z] = row_choice(rows, [(6, rank.astype(F32))], whole)[0:7]


def main_kernel(
    own, ext_ref, force_ref, energy_ref,
    frame_ref, size_ref, start_ref, left_ref, cell_ref, base_ref, dense_ref, dual_ref, count_ref, mine_ref, pool_ref,
    own_ref, acc_ref, pick_ref, wide_ref, spread_ref, table_ref, extra_cell_ref, extra_index_ref, copied,
):
    lx, ly, lz = own
    nx, ny, nz = lx + 2, ly + 2, lz + 2
    cx, cy, cz = lx + 1, ly + 1, lz + 1
    rows = rows_iota((8, 128))
    lane = lanes_iota((8, 128))
    zero = jnp.zeros((8, 128), F32)

    def tile_of(x, y, z):
        return (x * ny + y) * nz + z

    def cell_of(a, b, c):
        return (a * cy + b) * cz + c

    def mine_of(x, y, z):
        return ((x - 1) * ly + (y - 1)) * lz + (z - 1)

    def along(value, source):
        return jnp.take_along_axis(value, source, axis=1, mode="promise_in_bounds")

    def spread_row(ref, index, row):
        return jnp.broadcast_to(ref[index, row : row + 1], (8, 128))

    def right_rows(scaled):
        return row_choice(
            rows, [(3, 1.0 - norm_row(scaled)), (4, -1.0)], jnp.where(rows < 3, 2.0 * scaled, 0.0)
        )

    pick_rows = rows_iota((128, 512))
    pick_group = lanes_iota((128, 512)) // 128
    first_row = jnp.where(pick_group == 3, 51, pick_group)
    chosen = (pick_rows == first_row) | (pick_rows == first_row + 8) | (pick_rows == first_row + 32)
    pick_ref[...] = jnp.where(chosen, 1.0, 0.0).astype(BF16)

    @pl.loop(0, nx)
    def _(x):
        middle = jnp.where(rows == 0, x.astype(F32) - 0.5 * nx, 0.0)
        for y, z in [(y, z) for y in range(ny) for z in range(nz)]:
            tile = tile_of(x, y, z)
            feature = jnp.concatenate([ext_ref[tile], jnp.zeros((1, 128), F32)], axis=0)
            mask = jnp.where(feature[5:6] == rows.astype(F32), feature[3:4], 0.0)
            total = jnp.broadcast_to(jnp.sum(mask, axis=1, keepdims=True), (8, 128))
            size_ref[tile] = total.astype(jnp.int32)
            start_ref[tile] = sublane_exclusive(total, rows).astype(jnp.int32)
            offset = row_choice(rows, [(1, y - 0.5 * ny), (2, z - 0.5 * nz)], middle)
            scaled = (feature + offset) * INVERSE_CUTOFF
            frame_ref[tile] = jnp.where(rows < 3, scaled, feature)
            weight = feature[3:4] * (1.0 + CUBE_ROOT_STEP * feature[4:5])
            left = row_choice(rows, [(3, 1.0), (4, norm_row(scaled))], jnp.where(rows < 3, scaled, 0.0)) * weight
            stack = left_stack(left)
            full = jnp.concatenate([stack, pltpu.roll(stack, 64, 1), jnp.zeros((32, 128), F32)], axis=0)
            left_ref[tile] = full.astype(BF16).T[0:64]

    @pl.loop(0, cx)
    def _(a):
        for b, c in [(b, c) for b in range(cy) for c in range(cz)]:
            cell = cell_of(a, b, c)
            base = jnp.zeros((8, 128), jnp.int32)
            packed = zero
            for k, (bx, by, bz) in enumerate(OCTANTS):
                tile = tile_of(a + 1 - bx, b + 1 - by, c + 1 - bz)
                base_ref[cell, k] = base
                moved = along(frame_ref[tile], (lane + (spread_row(start_ref, tile, k) - base)) & 127)
                packed = jnp.where(lane >= base, moved, packed)
                base = base + spread_row(size_ref, tile, k)
            cell_ref[cell] = jnp.where(lane < base, packed, 0.0)
            count_ref[pl.ds(cell, 1)] = base[0:1]

    counting = pltpu.make_async_copy(count_ref, table_ref, copied)
    counting.start()

    def density_of(packed, tiles):
        stack = right_stack(right_rows(packed))
        right = block_diagonal(stack, stack)
        left = jnp.concatenate([left_ref[tile] for tile in tiles], axis=0)
        reach = jnp.maximum(jnp.dot(left, right, preferred_element_type=F32), 0.0)
        cube = reach * reach * reach
        acc = cube[0:8]
        for part in range(1, cube.shape[0] // 8):
            acc = acc + cube[8 * part : 8 * part + 8]
        both = acc[:, 0:128] + acc[:, 128:256]
        occupied, species = packed[3:4], packed[4:5]
        weight = occupied * (1.0 + DENSITY_STEP * species)
        density = jnp.sum(both, axis=0, keepdims=True) - weight
        slope = -0.5 * (occupied * (1.0 + EMBED_STEP * species)) / jnp.sqrt(1.0 + density)
        pair = occupied * (PAIR_BASE + PAIR_STEP * species)
        dual = row_choice(rows, [(3, weight), (4, pair), (5, slope)], packed)
        return jnp.broadcast_to(density, (8, 128)), dual

    @pl.loop(0, cx)
    def _(a):
        for b, c in [(b, c) for b in range(cy) for c in range(cz)]:
            cell = cell_of(a, b, c)
            tiles = [tile_of(a + 1 - bx, b + 1 - by, c + 1 - bz) for bx, by, bz in OCTANTS]
            dense_ref[cell], dual_ref[cell] = density_of(cell_ref[cell], tiles)

    counting.wait()
    extras = jnp.int32(0)
    most = jnp.int32(0)
    spilled = jnp.int32(0)
    for cell in range(cx * cy * cz):
        count = table_ref[cell, 0]
        extra_cell_ref[extras] = cell
        extra_index_ref[extras] = 1
        extras = extras + (count > 128).astype(jnp.int32)
        most = jnp.maximum(most, count)
        spilled = spilled + jnp.maximum(count - 128, 0)
    for x in range(1, lx + 1):
        for y in range(1, ly + 1):
            for z in range(1, lz + 1):
                tile = tile_of(x, y, z)
                density = zero
                for k, (bx, by, bz) in enumerate(OCTANTS):
                    cell = cell_of(x + bx - 1, y + by - 1, z + bz - 1)
                    start = spread_row(start_ref, tile, k)
                    moved = along(dense_ref[cell], (lane + (base_ref[cell, k] - start)) & 127)
                    density = jnp.where(lane >= start, moved, density)
                mine_ref[mine_of(x, y, z)] = density

    def more(cell, extras):
        def put(index, extras):
            extra_cell_ref[extras] = cell
            extra_index_ref[extras] = index
            return extras + 1

        return lax.fori_loop(2, (table_ref[cell, 0] + 127) // 128, put, extras)

    extras = lax.fori_loop(0, jnp.where(most > 256, cx * cy * cz, 0), more, extras)

    def around(cell):
        a = cell // (cy * cz)
        b = (cell // cz) % cy
        c = cell % cz
        return [(a + 1 - bx, b + 1 - by, c + 1 - bz) for bx, by, bz in OCTANTS]

    def own_tile(x, y, z):
        inside = (x >= 1) & (x <= lx) & (y >= 1) & (y <= ly) & (z >= 1) & (z <= lz)
        return inside, mine_of(x, y, z)

    pooled = spilled <= POOL
    pool_ref[...] = zero

    def extra_density(extra, offset):
        cell, index = extra_cell_ref[extra], extra_index_ref[extra]
        near = around(cell)
        tiles = [tile_of(*place) for place in near]
        packed = zero
        for k, tile in enumerate(tiles):
            place = lane + 128 * index - base_ref[cell, k]
            inside = (place >= 0) & (place < spread_row(size_ref, tile, k))
            moved = along(frame_ref[tile], (place + spread_row(start_ref, tile, k)) & 127)
            packed = jnp.where(inside, moved, packed)
        density, dual = density_of(packed, tiles)
        dual_ref[cx * cy * cz + extra] = dual
        held = jnp.minimum(table_ref[cell, 0] - 128 * index, 128)
        placed = (lane >= offset) & (lane < offset + held) & pooled
        pool_ref[...] = jnp.where(placed, along(dual, (lane - offset) & 127), pool_ref[...])
        for k, tile in enumerate(tiles):
            inside, mine = own_tile(*near[k])
            mine = jnp.where(inside, mine, lx * ly * lz)
            local = lane - spread_row(start_ref, tile, k)
            place = local + base_ref[cell, k] - 128 * index
            keep = (local >= 0) & (local < spread_row(size_ref, tile, k)) & (place >= 0) & (place < 128)
            mine_ref[mine] = jnp.where(keep, along(density, place & 127), mine_ref[mine])
        return offset + held

    lax.fori_loop(0, extras, extra_density, jnp.int32(0))

    def force_left(packed):
        pair = packed[4:5]
        left = row_choice(rows, [(3, 1.0), (4, norm_row(packed))], jnp.where(rows < 3, packed, 0.0))
        other = row_choice(rows, [(5, packed[3:4]), (6, packed[5:6])], left * pair)
        full = jnp.concatenate([left_stack(left), left_stack(other), jnp.zeros((32, 128), F32)], axis=0)
        return full.astype(BF16).T

    def spread_of(wide):
        return jnp.dot(wide, pick_ref[...], preferred_element_type=F32)

    def force_right(feature):
        right = right_rows(feature)
        mixed = row_choice(
            rows, [(5, feature[5:6]), (6, feature[3:4])], right * ((4.0 / 3.0) * feature[4:5])
        )
        return block_diagonal(right_stack(right), right_stack(mixed))

    def force_sums(slots, right, sums):
        sums = list(sums)
        left = jnp.concatenate([wide_ref[slot, 0:size] for slot, size in slots], axis=0)
        both = jnp.dot(left, right, preferred_element_type=F32)
        for k, (slot, size) in enumerate(slots):
            for part in range(size // 8):
                span = slice(8 * part, 8 * part + 8)
                whole = slice(128 * k + 8 * part, 128 * k + 8 * part + 8)
                reach = jnp.maximum(both[whole, 0:128], 0.0)
                square = reach * reach
                coef = square * both[whole, 128:256]
                for axis in range(3):
                    sums[axis] = sums[axis] + coef * spread_ref[slot, span, 128 * axis : 128 * axis + 128]
                sums[3] = sums[3] + square * square * spread_ref[slot, span, 384:512]
                sums[4] = sums[4] + coef
        return sums

    @pl.loop(0, cx)
    def _(a):
        plane = [a * (cy * cz) + k for k in range(cy * cz)]
        wides = [force_left(dual_ref[cell]) for cell in plane]
        spreads = spread_of(jnp.concatenate(wides, axis=0))
        for k, cell in enumerate(plane):
            wide_ref[cell] = wides[k]
            spread_ref[cell] = spreads[128 * k : 128 * k + 128]

    pool_wide = force_left(pool_ref[...])
    wide_ref[cx * cy * cz] = pool_wide
    spread_ref[cx * cy * cz, 0:POOL] = spread_of(pool_wide[0:POOL])

    @pl.loop(0, lx * ly)
    def _(column):
        x, y = column // ly + 1, column % ly + 1
        for z in range(1, lz + 1):
            mine = column * lz + z - 1
            feature = frame_ref[tile_of(x, y, z)]
            occupied, species = feature[3:4], feature[4:5]
            strength = occupied * (1.0 + EMBED_STEP * species)
            root = jnp.sqrt(1.0 + mine_ref[mine][0:1])
            feature = row_choice(
                rows,
                [
                    (3, occupied * (1.0 + DENSITY_STEP * species)),
                    (4, occupied * (PAIR_BASE + PAIR_STEP * species)),
                    (5, -0.5 * strength / root),
                    (6, -strength * root),
                ],
                feature,
            )
            own_ref[mine] = feature
            right = force_right(feature)
            slots = [(cell_of(x + bx - 1, y + by - 1, z + bz - 1), 128) for bx, by, bz in OCTANTS]
            slots.append((cx * cy * cz, POOL))
            for k, value in enumerate(force_sums(slots, right, [zero] * 5)):
                acc_ref[mine, k] = value

    @pl.loop(0, jnp.where(pooled, 0, extras))
    def _(extra):
        near = around(extra_cell_ref[extra])
        slot = cx * cy * cz
        wide_ref[slot] = force_left(dual_ref[slot + extra])
        spread_ref[slot] = spread_of(wide_ref[slot])
        for place in near:
            inside, mine = own_tile(*place)

            @pl.when(inside)
            def _():
                sums = force_sums([(slot, 128)], force_right(own_ref[mine]), [acc_ref[mine, k] for k in range(5)])
                for k in range(5):
                    acc_ref[mine, k] = sums[k]

    for x in range(lx):
        for y in range(ly):
            for z in range(lz):
                mine = (x * ly + y) * lz + z
                feature = own_ref[mine]
                parts = [jnp.sum(acc_ref[mine, k], axis=0, keepdims=True) for k in range(5)]
                pair = feature[4:5]
                energy = feature[6:7] + 0.5 * pair * (parts[3] - pair)
                scale = -6.0 / (CUTOFF_SQUARED * INVERSE_CUTOFF)
                result = row_choice(
                    rows,
                    [(k, (parts[k] - feature[k : k + 1] * parts[4]) * scale) for k in range(3)],
                    jnp.broadcast_to(energy, (8, 128)),
                )
                rank = ext_ref[tile_of(x + 1, y + 1, z + 1), 6:7].astype(jnp.int32)
                result = along(result, jnp.broadcast_to(rank, (8, 128)))
                for axis in range(3):
                    force_ref[axis, x, y, z : z + 1] = result[axis : axis + 1]
                energy_ref[x, y, z : z + 1] = result[3:4]


def extended(block, axis, dim, periodic):
    count = lax.axis_size(axis)
    size = block.shape[dim]
    first = lax.slice_in_dim(block, 0, 1, axis=dim)
    last = lax.slice_in_dim(block, size - 1, size, axis=dim)
    if periodic and count == 2 and size == 2:
        other = lax.ppermute(block, axis, [(0, 1), (1, 0)])
        low = lax.slice_in_dim(other, 1, 2, axis=dim)
        high = lax.slice_in_dim(other, 0, 1, axis=dim)
    elif count % 2 == 0:
        place = lax.axis_index(axis)
        even = place % 2 == 0
        inner = [(i, i ^ 1) for i in range(count)]
        outer = [(i, (i - 1 if i % 2 == 0 else i + 1) % count) for i in range(count)]
        if not periodic:
            outer[0], outer[-1] = (0, 0), (count - 1, count - 1)
        near = lax.ppermute(jnp.where(even, last, first), axis, inner)
        far = lax.ppermute(jnp.where(even, first, last), axis, outer)
        if not periodic:
            far = jnp.where((place == 0) | (place == count - 1), 0.0, far)
        low, high = jnp.where(even, far, near), jnp.where(even, near, far)
    else:
        forward = [(i, i + 1) for i in range(count - 1)]
        if periodic:
            forward.append((count - 1, 0))
        backward = [(target, source) for source, target in forward]
        low = lax.ppermute(last, axis, forward)
        high = lax.ppermute(first, axis, backward)
    return jnp.concatenate([low, block, high], axis=dim)


def shards(positions, species, counts):
    lx, ly, lz, width = species.shape
    own = (lx, ly, lz)
    mine = lx * ly * lz
    vmem = pl.BlockSpec(memory_space=pltpu.VMEM)
    block = pl.pallas_call(
        sort_kernel,
        out_shape=jax.ShapeDtypeStruct((lx, ly, lz, 7, width), F32),
        in_specs=[vmem, vmem, pl.BlockSpec(memory_space=pltpu.SMEM)],
        out_specs=vmem,
        name="sort",
    )(positions, species, counts)
    for axis, dim, periodic in (("gx", 0, True), ("gy", 1, True), ("gz", 2, False)):
        block = extended(block, axis, dim, periodic)
    tiles = (lx + 2) * (ly + 2) * (lz + 2)
    cells = (lx + 1) * (ly + 1) * (lz + 1)
    return pl.pallas_call(
        functools.partial(main_kernel, own),
        out_shape=(
            jax.ShapeDtypeStruct((3, lx, ly, lz, width), F32),
            jax.ShapeDtypeStruct((lx, ly, lz, width), F32),
        ),
        in_specs=[vmem],
        out_specs=(vmem, vmem),
        scratch_shapes=[
            pltpu.VMEM((tiles, 8, 128), F32),
            pltpu.VMEM((tiles, 8, 128), jnp.int32),
            pltpu.VMEM((tiles, 8, 128), jnp.int32),
            pltpu.VMEM((tiles, 64, 128), BF16),
            pltpu.VMEM((cells, 8, 128), F32),
            pltpu.VMEM((cells, 8, 8, 128), jnp.int32),
            pltpu.VMEM((cells, 8, 128), F32),
            pltpu.VMEM((cells + tiles, 8, 128), F32),
            pltpu.VMEM((cells, 128), jnp.int32),
            pltpu.VMEM((mine + 1, 8, 128), F32),
            pltpu.VMEM((8, 128), F32),
            pltpu.VMEM((mine, 8, 128), F32),
            pltpu.VMEM((mine, 5, 8, 128), F32),
            pltpu.VMEM((128, 512), BF16),
            pltpu.VMEM((cells + 1, 128, 128), BF16),
            pltpu.VMEM((cells + 1, 128, 512), F32),
            pltpu.SMEM((cells, 128), jnp.int32),
            pltpu.SMEM((tiles + 1,), jnp.int32),
            pltpu.SMEM((tiles + 1,), jnp.int32),
            pltpu.SemaphoreType.DMA,
        ],
        compiler_params=pltpu.CompilerParams(vmem_limit_bytes=32 << 20),
        name="atoms",
    )(block.reshape(tiles, 7, width))


def solution(mesh):
    placed = (P(None, "gx", "gy", "gz", None), P("gx", "gy", "gz", None), P("gx", "gy", "gz"))
    return jax.shard_map(
        shards,
        mesh=mesh,
        in_specs=placed,
        out_specs=(P(None, "gx", "gy", "gz", None), P("gx", "gy", "gz", None)),
        check_vma=False,
    )
```

```python
import functools

import jax
import jax.numpy as jnp
from jax import lax
from jax.experimental import pallas as pl
from jax.experimental.pallas import tpu as pltpu
from jax.sharding import PartitionSpec as P

CUTOFF_SQUARED = 0.2025
INVERSE_CUTOFF = 1.0 / 0.45
DENSITY_STEP = 0.4
CUBE_ROOT_STEP = 1.4 ** (1.0 / 3.0) - 1.0
EMBED_STEP = -0.3
LOWEST_LIMIT = 0.4505
HIGHEST_LIMIT = 0.5495
POOL = 32
PAIR_BASE = 0.6
PAIR_STEP = 0.3

F32 = jnp.float32
BF16 = jnp.bfloat16
OCTANTS = [(bx, by, bz) for bx in (0, 1) for by in (0, 1) for bz in (0, 1)]


def rows_iota(shape):
    return lax.broadcasted_iota(jnp.int32, shape, 0)


def lanes_iota(shape):
    return lax.broadcasted_iota(jnp.int32, shape, 1)


def split_three(value):
    first = value.astype(BF16).astype(F32)
    rest = value - first
    second = rest.astype(BF16).astype(F32)
    third = (rest - second).astype(BF16).astype(F32)
    return first, second, third


def left_stack(value):
    one, two, three = split_three(value)
    return jnp.concatenate([one, two, one, two, three, one], axis=0)


def right_stack(value):
    one, two, three = split_three(value)
    return jnp.concatenate([one, one, two, two, one, three], axis=0)


def block_diagonal(first, second):
    depth = first.shape[0]
    zero = jnp.zeros_like(first)
    pad = jnp.zeros((128 - 2 * depth, 256), F32)
    top = jnp.concatenate([first, zero], axis=1)
    low = jnp.concatenate([zero, second], axis=1)
    return jnp.concatenate([top, low, pad], axis=0).astype(BF16)


def row_choice(rows, pairs, other):
    for row, value in pairs:
        other = jnp.where(rows == row, value, other)
    return other


def norm_row(value):
    square = value * value
    return square[0:1] + square[1:2] + square[2:3]


def halves(value, group, limits, order):
    below = jnp.sum(jnp.where(value < limits, group, 0.0), axis=1, keepdims=True)
    total = jnp.sum(group, axis=1, keepdims=True)
    score = jnp.abs(2.0 * below - total) * 8.0 + order
    best = jnp.min(score, axis=0, keepdims=True)
    limit = jnp.max(jnp.where(score == best, limits, 0.0), axis=0, keepdims=True)
    return jnp.where(value >= limit, group, 0.0), jnp.where(value >= limit, 0.0, group)


def sublane_exclusive(value, rows):
    total = value
    for step in (1, 2, 4):
        total = total + jnp.where(rows >= step, pltpu.roll(total, step, 0), 0.0)
    return total - value


def sort_kernel(position_ref, species_ref, count_ref, sorted_ref):
    lx, ly, lz, _ = species_ref.shape
    rows = rows_iota((8, 128))
    wide_rows = rows_iota((128, 128))
    wide_lanes = lanes_iota((128, 128))
    triangle = jnp.where(wide_rows <= wide_lanes, 1.0, 0.0).astype(BF16)
    lane = lanes_iota((1, 128))
    order = rows.astype(F32)
    limits = LOWEST_LIMIT + (HIGHEST_LIMIT - LOWEST_LIMIT) / 7.0 * order
    for x in range(lx):
        for y in range(ly):
            for z in range(lz):
                occupied = jnp.where(lane < count_ref[x, y, z], 1.0, 0.0)
                groups = [jnp.broadcast_to(occupied, (8, 128))]
                for k in range(3):
                    value = jnp.broadcast_to(position_ref[k, x, y, z : z + 1], (8, 128))
                    pairs = [halves(value, group, limits, order) for group in groups]
                    groups = [part for high, low in pairs for part in (low, high)]
                mask = row_choice(rows, list(enumerate(groups))[1:], groups[0])
                octant = jnp.sum(mask * order, axis=0, keepdims=True)
                feature = row_choice(
                    rows,
                    [(k, position_ref[k, x, y, z : z + 1]) for k in range(3)]
                    + [(3, occupied), (4, species_ref[x, y, z : z + 1].astype(F32)), (5, octant)],
                    jnp.zeros((8, 128), F32),
                )
                prefix = jnp.dot(mask.astype(BF16), triangle, preferred_element_type=F32)
                total = jnp.broadcast_to(jnp.sum(mask, axis=1, keepdims=True), (8, 128))
                start = sublane_exclusive(total, rows)
                place = jnp.sum(mask * (prefix - 1.0 + start), axis=0, keepdims=True)
                rank = jnp.where(occupied > 0.5, place.astype(jnp.int32), lane)
                chosen = jnp.where(jnp.broadcast_to(rank, (128, 128)) == wide_rows, 1.0, 0.0).astype(BF16)
                one, two, three = split_three(feature)
                pieces = jnp.concatenate([one, two, three, jnp.zeros_like(one)], axis=0).astype(BF16)
                moved = lax.dot_general(
                    pieces, chosen, (((1,), (1,)), ((), ())), preferred_element_type=F32
                )
                whole = (moved[16:24] + moved[8:16]) + moved[0:8]
                sorted_ref[x, y, z] = row_choice(rows, [(6, rank.astype(F32))], whole)[0:7]


def main_kernel(
    own, ext_ref, force_ref, energy_ref,
    frame_ref, size_ref, start_ref, left_ref, cell_ref, base_ref, dense_ref, dual_ref, count_ref, mine_ref, pool_ref,
    own_ref, acc_ref, pick_ref, wide_ref, spread_ref, table_ref, extra_cell_ref, extra_index_ref, copied,
):
    lx, ly, lz = own
    nx, ny, nz = lx + 2, ly + 2, lz + 2
    cx, cy, cz = lx + 1, ly + 1, lz + 1
    rows = rows_iota((8, 128))
    lane = lanes_iota((8, 128))
    zero = jnp.zeros((8, 128), F32)

    def tile_of(x, y, z):
        return (x * ny + y) * nz + z

    def cell_of(a, b, c):
        return (a * cy + b) * cz + c

    def mine_of(x, y, z):
        return ((x - 1) * ly + (y - 1)) * lz + (z - 1)

    def along(value, source):
        return jnp.take_along_axis(value, source, axis=1, mode="promise_in_bounds")

    def spread_row(ref, index, row):
        return jnp.broadcast_to(ref[index, row : row + 1], (8, 128))

    def right_rows(scaled):
        return row_choice(
            rows, [(3, 1.0 - norm_row(scaled)), (4, -1.0)], jnp.where(rows < 3, 2.0 * scaled, 0.0)
        )

    pick_rows = rows_iota((128, 512))
    pick_group = lanes_iota((128, 512)) // 128
    first_row = jnp.where(pick_group == 3, 51, pick_group)
    chosen = (pick_rows == first_row) | (pick_rows == first_row + 8) | (pick_rows == first_row + 32)
    pick_ref[...] = jnp.where(chosen, 1.0, 0.0).astype(BF16)

    @pl.loop(0, nx)
    def _(x):
        middle = jnp.where(rows == 0, x.astype(F32) - 0.5 * nx, 0.0)
        for y, z in [(y, z) for y in range(ny) for z in range(nz)]:
            tile = tile_of(x, y, z)
            feature = jnp.concatenate([ext_ref[tile], jnp.zeros((1, 128), F32)], axis=0)
            mask = jnp.where(feature[5:6] == rows.astype(F32), feature[3:4], 0.0)
            total = jnp.broadcast_to(jnp.sum(mask, axis=1, keepdims=True), (8, 128))
            size_ref[tile] = total.astype(jnp.int32)
            start_ref[tile] = sublane_exclusive(total, rows).astype(jnp.int32)
            offset = row_choice(rows, [(1, y - 0.5 * ny), (2, z - 0.5 * nz)], middle)
            scaled = (feature + offset) * INVERSE_CUTOFF
            frame_ref[tile] = jnp.where(rows < 3, scaled, feature)
            weight = feature[3:4] * (1.0 + CUBE_ROOT_STEP * feature[4:5])
            left = row_choice(rows, [(3, 1.0), (4, norm_row(scaled))], jnp.where(rows < 3, scaled, 0.0)) * weight
            left_ref[tile] = jnp.concatenate([left_stack(left), jnp.zeros((80, 128), F32)], axis=0).astype(BF16)

    @pl.loop(0, cx)
    def _(a):
        for b, c in [(b, c) for b in range(cy) for c in range(cz)]:
            cell = cell_of(a, b, c)
            base = jnp.zeros((8, 128), jnp.int32)
            packed = zero
            for k, (bx, by, bz) in enumerate(OCTANTS):
                tile = tile_of(a + 1 - bx, b + 1 - by, c + 1 - bz)
                base_ref[cell, k] = base
                moved = along(frame_ref[tile], (lane + (spread_row(start_ref, tile, k) - base)) & 127)
                packed = jnp.where(lane >= base, moved, packed)
                base = base + spread_row(size_ref, tile, k)
            cell_ref[cell] = jnp.where(lane < base, packed, 0.0)
            count_ref[pl.ds(cell, 1)] = base[0:1]

    counting = pltpu.make_async_copy(count_ref, table_ref, copied)
    counting.start()

    def density_of(packed, tiles):
        stack = jnp.concatenate([right_stack(right_rows(packed)), jnp.zeros((80, 128), F32)], axis=0)
        turned = stack.astype(BF16).T
        groups = [zero] * 16
        for k in range(0, 8, 2):
            right = jnp.concatenate([left_ref[tiles[k]], left_ref[tiles[k + 1]]], axis=1)
            reach = jnp.maximum(jnp.dot(turned, right, preferred_element_type=F32), 0.0)
            cube = reach * reach * reach
            for g in range(16):
                part = cube[8 * g : 8 * g + 8]
                groups[g] = groups[g] + part[:, 0:128] + part[:, 128:256]
        both = zero
        for g in range(16):
            total = jnp.sum(groups[g], axis=1, keepdims=True)
            both = jnp.where(lane == rows + 8 * g, total, both)
        occupied, species = packed[3:4], packed[4:5]
        weight = occupied * (1.0 + DENSITY_STEP * species)
        density = jnp.sum(both, axis=0, keepdims=True) - weight
        slope = -0.5 * (occupied * (1.0 + EMBED_STEP * species)) / jnp.sqrt(1.0 + density)
        pair = occupied * (PAIR_BASE + PAIR_STEP * species)
        dual = row_choice(rows, [(3, weight), (4, pair), (5, slope)], packed)
        return jnp.broadcast_to(density, (8, 128)), dual

    @pl.loop(0, cx)
    def _(a):
        for b, c in [(b, c) for b in range(cy) for c in range(cz)]:
            cell = cell_of(a, b, c)
            tiles = [tile_of(a + 1 - bx, b + 1 - by, c + 1 - bz) for bx, by, bz in OCTANTS]
            dense_ref[cell], dual_ref[cell] = density_of(cell_ref[cell], tiles)

    counting.wait()
    extras = jnp.int32(0)
    most = jnp.int32(0)
    spilled = jnp.int32(0)
    for cell in range(cx * cy * cz):
        count = table_ref[cell, 0]
        extra_cell_ref[extras] = cell
        extra_index_ref[extras] = 1
        extras = extras + (count > 128).astype(jnp.int32)
        most = jnp.maximum(most, count)
        spilled = spilled + jnp.maximum(count - 128, 0)
    for x in range(1, lx + 1):
        for y in range(1, ly + 1):
            for z in range(1, lz + 1):
                tile = tile_of(x, y, z)
                density = zero
                for k, (bx, by, bz) in enumerate(OCTANTS):
                    cell = cell_of(x + bx - 1, y + by - 1, z + bz - 1)
                    start = spread_row(start_ref, tile, k)
                    moved = along(dense_ref[cell], (lane + (base_ref[cell, k] - start)) & 127)
                    density = jnp.where(lane >= start, moved, density)
                mine_ref[mine_of(x, y, z)] = density

    def more(cell, extras):
        def put(index, extras):
            extra_cell_ref[extras] = cell
            extra_index_ref[extras] = index
            return extras + 1

        return lax.fori_loop(2, (table_ref[cell, 0] + 127) // 128, put, extras)

    extras = lax.fori_loop(0, jnp.where(most > 256, cx * cy * cz, 0), more, extras)

    def around(cell):
        a = cell // (cy * cz)
        b = (cell // cz) % cy
        c = cell % cz
        return [(a + 1 - bx, b + 1 - by, c + 1 - bz) for bx, by, bz in OCTANTS]

    def own_tile(x, y, z):
        inside = (x >= 1) & (x <= lx) & (y >= 1) & (y <= ly) & (z >= 1) & (z <= lz)
        return inside, mine_of(x, y, z)

    pooled = spilled <= POOL
    pool_ref[...] = zero

    def extra_density(extra, offset):
        cell, index = extra_cell_ref[extra], extra_index_ref[extra]
        near = around(cell)
        tiles = [tile_of(*place) for place in near]
        packed = zero
        for k, tile in enumerate(tiles):
            place = lane + 128 * index - base_ref[cell, k]
            inside = (place >= 0) & (place < spread_row(size_ref, tile, k))
            moved = along(frame_ref[tile], (place + spread_row(start_ref, tile, k)) & 127)
            packed = jnp.where(inside, moved, packed)
        density, dual = density_of(packed, tiles)
        dual_ref[cx * cy * cz + extra] = dual
        held = jnp.minimum(table_ref[cell, 0] - 128 * index, 128)
        placed = (lane >= offset) & (lane < offset + held) & pooled
        pool_ref[...] = jnp.where(placed, along(dual, (lane - offset) & 127), pool_ref[...])
        for k, tile in enumerate(tiles):
            inside, mine = own_tile(*near[k])
            mine = jnp.where(inside, mine, lx * ly * lz)
            local = lane - spread_row(start_ref, tile, k)
            place = local + base_ref[cell, k] - 128 * index
            keep = (local >= 0) & (local < spread_row(size_ref, tile, k)) & (place >= 0) & (place < 128)
            mine_ref[mine] = jnp.where(keep, along(density, place & 127), mine_ref[mine])
        return offset + held

    lax.fori_loop(0, extras, extra_density, jnp.int32(0))

    def force_left(packed):
        pair = packed[4:5]
        left = row_choice(rows, [(3, 1.0), (4, norm_row(packed))], jnp.where(rows < 3, packed, 0.0))
        other = row_choice(rows, [(5, packed[3:4]), (6, packed[5:6])], left * pair)
        full = jnp.concatenate([left_stack(left), left_stack(other), jnp.zeros((32, 128), F32)], axis=0)
        return full.astype(BF16).T

    def spread_of(wide):
        return jnp.dot(wide, pick_ref[...], preferred_element_type=F32)

    def force_right(feature):
        right = right_rows(feature)
        mixed = row_choice(
            rows, [(5, feature[5:6]), (6, feature[3:4])], right * ((4.0 / 3.0) * feature[4:5])
        )
        return block_diagonal(right_stack(right), right_stack(mixed))

    def force_sums(slots, right, sums):
        sums = list(sums)
        left = jnp.concatenate([wide_ref[slot, 0:size] for slot, size in slots], axis=0)
        both = jnp.dot(left, right, preferred_element_type=F32)
        for k, (slot, size) in enumerate(slots):
            for part in range(size // 8):
                span = slice(8 * part, 8 * part + 8)
                whole = slice(128 * k + 8 * part, 128 * k + 8 * part + 8)
                reach = jnp.maximum(both[whole, 0:128], 0.0)
                square = reach * reach
                coef = square * both[whole, 128:256]
                for axis in range(3):
                    sums[axis] = sums[axis] + coef * spread_ref[slot, span, 128 * axis : 128 * axis + 128]
                sums[3] = sums[3] + square * square * spread_ref[slot, span, 384:512]
                sums[4] = sums[4] + coef
        return sums

    @pl.loop(0, cx)
    def _(a):
        plane = [a * (cy * cz) + k for k in range(cy * cz)]
        wides = [force_left(dual_ref[cell]) for cell in plane]
        spreads = spread_of(jnp.concatenate(wides, axis=0))
        for k, cell in enumerate(plane):
            wide_ref[cell] = wides[k]
            spread_ref[cell] = spreads[128 * k : 128 * k + 128]

    pool_wide = force_left(pool_ref[...])
    wide_ref[cx * cy * cz] = pool_wide
    spread_ref[cx * cy * cz, 0:POOL] = spread_of(pool_wide[0:POOL])

    @pl.loop(0, lx * ly)
    def _(column):
        x, y = column // ly + 1, column % ly + 1
        for z in range(1, lz + 1):
            mine = column * lz + z - 1
            feature = frame_ref[tile_of(x, y, z)]
            occupied, species = feature[3:4], feature[4:5]
            strength = occupied * (1.0 + EMBED_STEP * species)
            root = jnp.sqrt(1.0 + mine_ref[mine][0:1])
            feature = row_choice(
                rows,
                [
                    (3, occupied * (1.0 + DENSITY_STEP * species)),
                    (4, occupied * (PAIR_BASE + PAIR_STEP * species)),
                    (5, -0.5 * strength / root),
                    (6, -strength * root),
                ],
                feature,
            )
            own_ref[mine] = feature
            right = force_right(feature)
            slots = [(cell_of(x + bx - 1, y + by - 1, z + bz - 1), 128) for bx, by, bz in OCTANTS]
            slots.append((cx * cy * cz, POOL))
            for k, value in enumerate(force_sums(slots, right, [zero] * 5)):
                acc_ref[mine, k] = value

    @pl.loop(0, jnp.where(pooled, 0, extras))
    def _(extra):
        near = around(extra_cell_ref[extra])
        slot = cx * cy * cz
        wide_ref[slot] = force_left(dual_ref[slot + extra])
        spread_ref[slot] = spread_of(wide_ref[slot])
        for place in near:
            inside, mine = own_tile(*place)

            @pl.when(inside)
            def _():
                sums = force_sums([(slot, 128)], force_right(own_ref[mine]), [acc_ref[mine, k] for k in range(5)])
                for k in range(5):
                    acc_ref[mine, k] = sums[k]

    for x in range(lx):
        for y in range(ly):
            for z in range(lz):
                mine = (x * ly + y) * lz + z
                feature = own_ref[mine]
                parts = [jnp.sum(acc_ref[mine, k], axis=0, keepdims=True) for k in range(5)]
                pair = feature[4:5]
                energy = feature[6:7] + 0.5 * pair * (parts[3] - pair)
                scale = -6.0 / (CUTOFF_SQUARED * INVERSE_CUTOFF)
                result = row_choice(
                    rows,
                    [(k, (parts[k] - feature[k : k + 1] * parts[4]) * scale) for k in range(3)],
                    jnp.broadcast_to(energy, (8, 128)),
                )
                rank = ext_ref[tile_of(x + 1, y + 1, z + 1), 6:7].astype(jnp.int32)
                result = along(result, jnp.broadcast_to(rank, (8, 128)))
                for axis in range(3):
                    force_ref[axis, x, y, z : z + 1] = result[axis : axis + 1]
                energy_ref[x, y, z : z + 1] = result[3:4]


def extended(block, axis, dim, periodic):
    count = lax.axis_size(axis)
    size = block.shape[dim]
    first = lax.slice_in_dim(block, 0, 1, axis=dim)
    last = lax.slice_in_dim(block, size - 1, size, axis=dim)
    if periodic and count == 2 and size == 2:
        other = lax.ppermute(block, axis, [(0, 1), (1, 0)])
        low = lax.slice_in_dim(other, 1, 2, axis=dim)
        high = lax.slice_in_dim(other, 0, 1, axis=dim)
    elif count % 2 == 0:
        place = lax.axis_index(axis)
        even = place % 2 == 0
        inner = [(i, i ^ 1) for i in range(count)]
        outer = [(i, (i - 1 if i % 2 == 0 else i + 1) % count) for i in range(count)]
        if not periodic:
            outer[0], outer[-1] = (0, 0), (count - 1, count - 1)
        near = lax.ppermute(jnp.where(even, last, first), axis, inner)
        far = lax.ppermute(jnp.where(even, first, last), axis, outer)
        if not periodic:
            far = jnp.where((place == 0) | (place == count - 1), 0.0, far)
        low, high = jnp.where(even, far, near), jnp.where(even, near, far)
    else:
        forward = [(i, i + 1) for i in range(count - 1)]
        if periodic:
            forward.append((count - 1, 0))
        backward = [(target, source) for source, target in forward]
        low = lax.ppermute(last, axis, forward)
        high = lax.ppermute(first, axis, backward)
    return jnp.concatenate([low, block, high], axis=dim)


def shards(positions, species, counts):
    lx, ly, lz, width = species.shape
    own = (lx, ly, lz)
    mine = lx * ly * lz
    vmem = pl.BlockSpec(memory_space=pltpu.VMEM)
    block = pl.pallas_call(
        sort_kernel,
        out_shape=jax.ShapeDtypeStruct((lx, ly, lz, 7, width), F32),
        in_specs=[vmem, vmem, pl.BlockSpec(memory_space=pltpu.SMEM)],
        out_specs=vmem,
        name="sort",
    )(positions, species, counts)
    for axis, dim, periodic in (("gx", 0, True), ("gy", 1, True), ("gz", 2, False)):
        block = extended(block, axis, dim, periodic)
    tiles = (lx + 2) * (ly + 2) * (lz + 2)
    cells = (lx + 1) * (ly + 1) * (lz + 1)
    return pl.pallas_call(
        functools.partial(main_kernel, own),
        out_shape=(
            jax.ShapeDtypeStruct((3, lx, ly, lz, width), F32),
            jax.ShapeDtypeStruct((lx, ly, lz, width), F32),
        ),
        in_specs=[vmem],
        out_specs=(vmem, vmem),
        scratch_shapes=[
            pltpu.VMEM((tiles, 8, 128), F32),
            pltpu.VMEM((tiles, 8, 128), jnp.int32),
            pltpu.VMEM((tiles, 8, 128), jnp.int32),
            pltpu.VMEM((tiles, 128, 128), BF16),
            pltpu.VMEM((cells, 8, 128), F32),
            pltpu.VMEM((cells, 8, 8, 128), jnp.int32),
            pltpu.VMEM((cells, 8, 128), F32),
            pltpu.VMEM((cells + tiles, 8, 128), F32),
            pltpu.VMEM((cells, 128), jnp.int32),
            pltpu.VMEM((mine + 1, 8, 128), F32),
            pltpu.VMEM((8, 128), F32),
            pltpu.VMEM((mine, 8, 128), F32),
            pltpu.VMEM((mine, 5, 8, 128), F32),
            pltpu.VMEM((128, 512), BF16),
            pltpu.VMEM((cells + 1, 128, 128), BF16),
            pltpu.VMEM((cells + 1, 128, 512), F32),
            pltpu.SMEM((cells, 128), jnp.int32),
            pltpu.SMEM((tiles + 1,), jnp.int32),
            pltpu.SMEM((tiles + 1,), jnp.int32),
            pltpu.SemaphoreType.DMA,
        ],
        compiler_params=pltpu.CompilerParams(vmem_limit_bytes=32 << 20),
        name="atoms",
    )(block.reshape(tiles, 7, width))


def solution(mesh):
    placed = (P(None, "gx", "gy", "gz", None), P("gx", "gy", "gz", None), P("gx", "gy", "gz"))
    return jax.shard_map(
        shards,
        mesh=mesh,
        in_specs=placed,
        out_specs=(P(None, "gx", "gy", "gz", None), P("gx", "gy", "gz", None)),
        check_vma=False,
    )
```

```python
import functools

import jax
import jax.numpy as jnp
from jax import lax
from jax.experimental import pallas as pl
from jax.experimental.pallas import tpu as pltpu
from jax.sharding import PartitionSpec as P

CUTOFF_SQUARED = 0.2025
INVERSE_CUTOFF = 1.0 / 0.45
DENSITY_STEP = 0.4
CUBE_ROOT_STEP = 1.4 ** (1.0 / 3.0) - 1.0
EMBED_STEP = -0.3
LOWEST_LIMIT = 0.4505
HIGHEST_LIMIT = 0.5495
POOL = 32
PAIR_BASE = 0.6
PAIR_STEP = 0.3

F32 = jnp.float32
BF16 = jnp.bfloat16
OCTANTS = [(bx, by, bz) for bx in (0, 1) for by in (0, 1) for bz in (0, 1)]


def rows_iota(shape):
    return lax.broadcasted_iota(jnp.int32, shape, 0)


def lanes_iota(shape):
    return lax.broadcasted_iota(jnp.int32, shape, 1)


def split_three(value):
    first = value.astype(BF16).astype(F32)
    rest = value - first
    second = rest.astype(BF16).astype(F32)
    third = (rest - second).astype(BF16).astype(F32)
    return first, second, third


def left_stack(value):
    one, two, three = split_three(value)
    return jnp.concatenate([one, two, one, two, three, one], axis=0)


def right_stack(value):
    one, two, three = split_three(value)
    return jnp.concatenate([one, one, two, two, one, three], axis=0)


def block_diagonal(first, second):
    depth = first.shape[0]
    zero = jnp.zeros_like(first)
    pad = jnp.zeros((128 - 2 * depth, 256), F32)
    top = jnp.concatenate([first, zero], axis=1)
    low = jnp.concatenate([zero, second], axis=1)
    return jnp.concatenate([top, low, pad], axis=0).astype(BF16)


def row_choice(rows, pairs, other):
    for row, value in pairs:
        other = jnp.where(rows == row, value, other)
    return other


def norm_row(value):
    square = value * value
    return square[0:1] + square[1:2] + square[2:3]


def halves(value, group, limits, order):
    below = jnp.sum(jnp.where(value < limits, group, 0.0), axis=1, keepdims=True)
    total = jnp.sum(group, axis=1, keepdims=True)
    score = jnp.abs(2.0 * below - total) * 8.0 + order
    best = jnp.min(score, axis=0, keepdims=True)
    limit = jnp.max(jnp.where(score == best, limits, 0.0), axis=0, keepdims=True)
    return jnp.where(value >= limit, group, 0.0), jnp.where(value >= limit, 0.0, group)


def sublane_exclusive(value, rows):
    total = value
    for step in (1, 2, 4):
        total = total + jnp.where(rows >= step, pltpu.roll(total, step, 0), 0.0)
    return total - value


def sort_kernel(position_ref, species_ref, count_ref, sorted_ref):
    lx, ly, lz, _ = species_ref.shape
    rows = rows_iota((8, 128))
    wide_rows = rows_iota((128, 128))
    wide_lanes = lanes_iota((128, 128))
    triangle = jnp.where(wide_rows <= wide_lanes, 1.0, 0.0).astype(BF16)
    lane = lanes_iota((1, 128))
    order = rows.astype(F32)
    limits = LOWEST_LIMIT + (HIGHEST_LIMIT - LOWEST_LIMIT) / 7.0 * order
    for x in range(lx):
        for y in range(ly):
            for z in range(lz):
                occupied = jnp.where(lane < count_ref[x, y, z], 1.0, 0.0)
                groups = [jnp.broadcast_to(occupied, (8, 128))]
                for k in range(3):
                    value = jnp.broadcast_to(position_ref[k, x, y, z : z + 1], (8, 128))
                    pairs = [halves(value, group, limits, order) for group in groups]
                    groups = [part for high, low in pairs for part in (low, high)]
                mask = row_choice(rows, list(enumerate(groups))[1:], groups[0])
                octant = jnp.sum(mask * order, axis=0, keepdims=True)
                feature = row_choice(
                    rows,
                    [(k, position_ref[k, x, y, z : z + 1]) for k in range(3)]
                    + [(3, occupied), (4, species_ref[x, y, z : z + 1].astype(F32)), (5, octant)],
                    jnp.zeros((8, 128), F32),
                )
                prefix = jnp.dot(mask.astype(BF16), triangle, preferred_element_type=F32)
                total = jnp.broadcast_to(jnp.sum(mask, axis=1, keepdims=True), (8, 128))
                start = sublane_exclusive(total, rows)
                place = jnp.sum(mask * (prefix - 1.0 + start), axis=0, keepdims=True)
                rank = jnp.where(occupied > 0.5, place.astype(jnp.int32), lane)
                chosen = jnp.where(jnp.broadcast_to(rank, (128, 128)) == wide_rows, 1.0, 0.0).astype(BF16)
                one, two, three = split_three(feature)
                pieces = jnp.concatenate([one, two, three, jnp.zeros_like(one)], axis=0).astype(BF16)
                moved = lax.dot_general(
                    pieces, chosen, (((1,), (1,)), ((), ())), preferred_element_type=F32
                )
                whole = (moved[16:24] + moved[8:16]) + moved[0:8]
                sorted_ref[x, y, z] = row_choice(rows, [(6, rank.astype(F32))], whole)[0:7]


def main_kernel(
    own, ext_ref, force_ref, energy_ref,
    frame_ref, size_ref, start_ref, left_ref, cell_ref, base_ref, dense_ref, dual_ref, count_ref, mine_ref, pool_ref,
    own_ref, acc_ref, pick_ref, wide_ref, spare_ref, spread_ref, table_ref, extra_cell_ref, extra_index_ref, copied,
):
    lx, ly, lz = own
    nx, ny, nz = lx + 2, ly + 2, lz + 2
    cx, cy, cz = lx + 1, ly + 1, lz + 1
    rows = rows_iota((8, 128))
    lane = lanes_iota((8, 128))
    zero = jnp.zeros((8, 128), F32)

    def tile_of(x, y, z):
        return (x * ny + y) * nz + z

    def cell_of(a, b, c):
        return (a * cy + b) * cz + c

    def mine_of(x, y, z):
        return ((x - 1) * ly + (y - 1)) * lz + (z - 1)

    def along(value, source):
        return jnp.take_along_axis(value, source, axis=1, mode="promise_in_bounds")

    def spread_row(ref, index, row):
        return jnp.broadcast_to(ref[index, row : row + 1], (8, 128))

    def right_rows(scaled):
        return row_choice(
            rows, [(3, 1.0 - norm_row(scaled)), (4, -1.0)], jnp.where(rows < 3, 2.0 * scaled, 0.0)
        )

    pick_rows = rows_iota((128, 512))
    pick_group = lanes_iota((128, 512)) // 128
    first_row = jnp.where(pick_group == 3, 51, pick_group)
    chosen = (pick_rows == first_row) | (pick_rows == first_row + 8) | (pick_rows == first_row + 32)
    pick_ref[...] = jnp.where(chosen, 1.0, 0.0).astype(BF16)

    @pl.loop(0, nx)
    def _(x):
        middle = jnp.where(rows == 0, x.astype(F32) - 0.5 * nx, 0.0)
        for y, z in [(y, z) for y in range(ny) for z in range(nz)]:
            tile = tile_of(x, y, z)
            feature = jnp.concatenate([ext_ref[tile], jnp.zeros((1, 128), F32)], axis=0)
            mask = jnp.where(feature[5:6] == rows.astype(F32), feature[3:4], 0.0)
            total = jnp.broadcast_to(jnp.sum(mask, axis=1, keepdims=True), (8, 128))
            size_ref[tile] = total.astype(jnp.int32)
            start_ref[tile] = sublane_exclusive(total, rows).astype(jnp.int32)
            offset = row_choice(rows, [(1, y - 0.5 * ny), (2, z - 0.5 * nz)], middle)
            scaled = (feature + offset) * INVERSE_CUTOFF
            frame_ref[tile] = jnp.where(rows < 3, scaled, feature)
            weight = feature[3:4] * (1.0 + CUBE_ROOT_STEP * feature[4:5])
            left = row_choice(rows, [(3, 1.0), (4, norm_row(scaled))], jnp.where(rows < 3, scaled, 0.0)) * weight
            left_ref[tile] = jnp.concatenate([left_stack(left), jnp.zeros((80, 128), F32)], axis=0).astype(BF16)

    @pl.loop(0, cx)
    def _(a):
        for b, c in [(b, c) for b in range(cy) for c in range(cz)]:
            cell = cell_of(a, b, c)
            base = jnp.zeros((8, 128), jnp.int32)
            packed = zero
            for k, (bx, by, bz) in enumerate(OCTANTS):
                tile = tile_of(a + 1 - bx, b + 1 - by, c + 1 - bz)
                base_ref[cell, k] = base
                moved = along(frame_ref[tile], (lane + (spread_row(start_ref, tile, k) - base)) & 127)
                packed = jnp.where(lane >= base, moved, packed)
                base = base + spread_row(size_ref, tile, k)
            cell_ref[cell] = jnp.where(lane < base, packed, 0.0)
            count_ref[pl.ds(cell, 1)] = base[0:1]

    counting = pltpu.make_async_copy(count_ref, table_ref, copied)
    counting.start()

    def density_of(packed, tiles):
        stack = jnp.concatenate([right_stack(right_rows(packed)), jnp.zeros((80, 128), F32)], axis=0)
        turned = stack.astype(BF16).T
        groups = [zero] * 16
        for k in range(0, 8, 2):
            right = jnp.concatenate([left_ref[tiles[k]], left_ref[tiles[k + 1]]], axis=1)
            reach = jnp.maximum(jnp.dot(turned, right, preferred_element_type=F32), 0.0)
            cube = reach * reach * reach
            for g in range(16):
                part = cube[8 * g : 8 * g + 8]
                groups[g] = groups[g] + part[:, 0:128] + part[:, 128:256]
        both = zero
        for g in range(16):
            total = jnp.sum(groups[g], axis=1, keepdims=True)
            both = jnp.where(lane == rows + 8 * g, total, both)
        occupied, species = packed[3:4], packed[4:5]
        weight = occupied * (1.0 + DENSITY_STEP * species)
        density = jnp.sum(both, axis=0, keepdims=True) - weight
        slope = -0.5 * (occupied * (1.0 + EMBED_STEP * species)) / jnp.sqrt(1.0 + density)
        pair = occupied * (PAIR_BASE + PAIR_STEP * species)
        dual = row_choice(rows, [(3, weight), (4, pair), (5, slope)], packed)
        return jnp.broadcast_to(density, (8, 128)), dual

    @pl.loop(0, cx)
    def _(a):
        for b, c in [(b, c) for b in range(cy) for c in range(cz)]:
            cell = cell_of(a, b, c)
            tiles = [tile_of(a + 1 - bx, b + 1 - by, c + 1 - bz) for bx, by, bz in OCTANTS]
            dense_ref[cell], dual_ref[cell] = density_of(cell_ref[cell], tiles)

    counting.wait()
    extras = jnp.int32(0)
    most = jnp.int32(0)
    spilled = jnp.int32(0)
    for cell in range(cx * cy * cz):
        count = table_ref[cell, 0]
        extra_cell_ref[extras] = cell
        extra_index_ref[extras] = 1
        extras = extras + (count > 128).astype(jnp.int32)
        most = jnp.maximum(most, count)
        spilled = spilled + jnp.maximum(count - 128, 0)
    for x in range(1, lx + 1):
        for y in range(1, ly + 1):
            for z in range(1, lz + 1):
                tile = tile_of(x, y, z)
                density = zero
                for k, (bx, by, bz) in enumerate(OCTANTS):
                    cell = cell_of(x + bx - 1, y + by - 1, z + bz - 1)
                    start = spread_row(start_ref, tile, k)
                    moved = along(dense_ref[cell], (lane + (base_ref[cell, k] - start)) & 127)
                    density = jnp.where(lane >= start, moved, density)
                mine_ref[mine_of(x, y, z)] = density

    def more(cell, extras):
        def put(index, extras):
            extra_cell_ref[extras] = cell
            extra_index_ref[extras] = index
            return extras + 1

        return lax.fori_loop(2, (table_ref[cell, 0] + 127) // 128, put, extras)

    extras = lax.fori_loop(0, jnp.where(most > 256, cx * cy * cz, 0), more, extras)

    def around(cell):
        a = cell // (cy * cz)
        b = (cell // cz) % cy
        c = cell % cz
        return [(a + 1 - bx, b + 1 - by, c + 1 - bz) for bx, by, bz in OCTANTS]

    def own_tile(x, y, z):
        inside = (x >= 1) & (x <= lx) & (y >= 1) & (y <= ly) & (z >= 1) & (z <= lz)
        return inside, mine_of(x, y, z)

    pooled = spilled <= POOL
    pool_ref[...] = zero

    def extra_density(extra, offset):
        cell, index = extra_cell_ref[extra], extra_index_ref[extra]
        near = around(cell)
        tiles = [tile_of(*place) for place in near]
        packed = zero
        for k, tile in enumerate(tiles):
            place = lane + 128 * index - base_ref[cell, k]
            inside = (place >= 0) & (place < spread_row(size_ref, tile, k))
            moved = along(frame_ref[tile], (place + spread_row(start_ref, tile, k)) & 127)
            packed = jnp.where(inside, moved, packed)
        density, dual = density_of(packed, tiles)
        dual_ref[cx * cy * cz + extra] = dual
        held = jnp.minimum(table_ref[cell, 0] - 128 * index, 128)
        placed = (lane >= offset) & (lane < offset + held) & pooled
        pool_ref[...] = jnp.where(placed, along(dual, (lane - offset) & 127), pool_ref[...])
        for k, tile in enumerate(tiles):
            inside, mine = own_tile(*near[k])
            mine = jnp.where(inside, mine, lx * ly * lz)
            local = lane - spread_row(start_ref, tile, k)
            place = local + base_ref[cell, k] - 128 * index
            keep = (local >= 0) & (local < spread_row(size_ref, tile, k)) & (place >= 0) & (place < 128)
            mine_ref[mine] = jnp.where(keep, along(density, place & 127), mine_ref[mine])
        return offset + held

    lax.fori_loop(0, extras, extra_density, jnp.int32(0))

    def force_stacks(packed):
        pair = packed[4:5]
        left = row_choice(rows, [(3, 1.0), (4, norm_row(packed))], jnp.where(rows < 3, packed, 0.0))
        other = row_choice(rows, [(5, packed[3:4]), (6, packed[5:6])], left * pair)
        return left_stack(left), left_stack(other)

    def force_left(packed):
        full = jnp.concatenate([*force_stacks(packed), jnp.zeros((32, 128), F32)], axis=0)
        return full.astype(BF16).T

    def spread_of(wide):
        return jnp.dot(wide, pick_ref[...], preferred_element_type=F32)

    def own_stacks(feature):
        right = right_rows(feature)
        mixed = row_choice(
            rows, [(5, feature[5:6]), (6, feature[3:4])], right * ((4.0 / 3.0) * feature[4:5])
        )
        return right_stack(right), right_stack(mixed)

    def add_terms(sums, reach, other, spreads):
        reach = jnp.maximum(reach, 0.0)
        square = reach * reach
        coef = square * other
        for axis in range(3):
            sums[axis] = sums[axis] + coef * spreads[axis]
        sums[3] = sums[3] + square * square * spreads[3]
        sums[4] = sums[4] + coef

    def spare_sums(size, right, sums):
        sums = list(sums)
        both = jnp.dot(spare_ref[0:size], right, preferred_element_type=F32)
        for part in range(size // 8):
            span = slice(8 * part, 8 * part + 8)
            spreads = [spread_ref[span, 128 * k : 128 * k + 128] for k in range(4)]
            add_terms(sums, both[span, 0:128], both[span, 128:256], spreads)
        return sums

    def cell_sums(slots, turned, half):
        groups = [[zero] * 5 for _ in range(4)]
        for slot in slots:
            both = jnp.dot(turned[32 * half : 32 * half + 32], wide_ref[slot], preferred_element_type=F32)
            spreads = [spread_row(dual_ref, slot, k) for k in (0, 1, 2, 4)]
            for g in range(4):
                part = both[8 * g : 8 * g + 8]
                add_terms(groups[g], part[:, 0:128], part[:, 128:256], spreads)
        return groups

    @pl.loop(0, cx)
    def _(a):
        for k in range(cy * cz):
            cell = a * (cy * cz) + k
            wide_ref[cell] = block_diagonal(*force_stacks(dual_ref[cell]))

    pool_wide = force_left(pool_ref[...])
    spare_ref[...] = pool_wide
    spread_ref[0:POOL] = spread_of(pool_wide[0:POOL])

    @pl.loop(0, lx * ly)
    def _(column):
        x, y = column // ly + 1, column % ly + 1
        for z in range(1, lz + 1):
            mine = column * lz + z - 1
            feature = frame_ref[tile_of(x, y, z)]
            occupied, species = feature[3:4], feature[4:5]
            strength = occupied * (1.0 + EMBED_STEP * species)
            root = jnp.sqrt(1.0 + mine_ref[mine][0:1])
            feature = row_choice(
                rows,
                [
                    (3, occupied * (1.0 + DENSITY_STEP * species)),
                    (4, occupied * (PAIR_BASE + PAIR_STEP * species)),
                    (5, -0.5 * strength / root),
                    (6, -strength * root),
                ],
                feature,
            )
            own_ref[mine] = feature
            stacks = own_stacks(feature)
            turned = jnp.concatenate([*stacks, jnp.zeros((32, 128), F32)], axis=0).astype(BF16).T
            slots = [cell_of(x + bx - 1, y + by - 1, z + bz - 1) for bx, by, bz in OCTANTS]
            sums = spare_sums(POOL, block_diagonal(*stacks), [zero] * 5)
            found = [zero] * 5
            for half in range(4):
                for g, group in enumerate(cell_sums(slots, turned, half)):
                    spot = lane == rows + (32 * half + 8 * g)
                    for k in range(5):
                        found[k] = jnp.where(spot, jnp.sum(group[k], axis=1, keepdims=True), found[k])
            for k in range(5):
                acc_ref[mine, k] = sums[k] + found[k]

    @pl.loop(0, jnp.where(pooled, 0, extras))
    def _(extra):
        near = around(extra_cell_ref[extra])
        spare_ref[...] = force_left(dual_ref[cx * cy * cz + extra])
        spread_ref[...] = spread_of(spare_ref[...])
        for place in near:
            inside, mine = own_tile(*place)

            @pl.when(inside)
            def _():
                right = block_diagonal(*own_stacks(own_ref[mine]))
                sums = spare_sums(128, right, [acc_ref[mine, k] for k in range(5)])
                for k in range(5):
                    acc_ref[mine, k] = sums[k]

    for x in range(lx):
        for y in range(ly):
            for z in range(lz):
                mine = (x * ly + y) * lz + z
                feature = own_ref[mine]
                parts = [jnp.sum(acc_ref[mine, k], axis=0, keepdims=True) for k in range(5)]
                pair = feature[4:5]
                energy = feature[6:7] + 0.5 * pair * (parts[3] - pair)
                scale = -6.0 / (CUTOFF_SQUARED * INVERSE_CUTOFF)
                result = row_choice(
                    rows,
                    [(k, (parts[k] - feature[k : k + 1] * parts[4]) * scale) for k in range(3)],
                    jnp.broadcast_to(energy, (8, 128)),
                )
                rank = ext_ref[tile_of(x + 1, y + 1, z + 1), 6:7].astype(jnp.int32)
                result = along(result, jnp.broadcast_to(rank, (8, 128)))
                for axis in range(3):
                    force_ref[axis, x, y, z : z + 1] = result[axis : axis + 1]
                energy_ref[x, y, z : z + 1] = result[3:4]


def extended(block, axis, dim, periodic):
    count = lax.axis_size(axis)
    size = block.shape[dim]
    first = lax.slice_in_dim(block, 0, 1, axis=dim)
    last = lax.slice_in_dim(block, size - 1, size, axis=dim)
    if periodic and count == 2 and size == 2:
        other = lax.ppermute(block, axis, [(0, 1), (1, 0)])
        low = lax.slice_in_dim(other, 1, 2, axis=dim)
        high = lax.slice_in_dim(other, 0, 1, axis=dim)
    elif count % 2 == 0:
        place = lax.axis_index(axis)
        even = place % 2 == 0
        inner = [(i, i ^ 1) for i in range(count)]
        outer = [(i, (i - 1 if i % 2 == 0 else i + 1) % count) for i in range(count)]
        if not periodic:
            outer[0], outer[-1] = (0, 0), (count - 1, count - 1)
        near = lax.ppermute(jnp.where(even, last, first), axis, inner)
        far = lax.ppermute(jnp.where(even, first, last), axis, outer)
        if not periodic:
            far = jnp.where((place == 0) | (place == count - 1), 0.0, far)
        low, high = jnp.where(even, far, near), jnp.where(even, near, far)
    else:
        forward = [(i, i + 1) for i in range(count - 1)]
        if periodic:
            forward.append((count - 1, 0))
        backward = [(target, source) for source, target in forward]
        low = lax.ppermute(last, axis, forward)
        high = lax.ppermute(first, axis, backward)
    return jnp.concatenate([low, block, high], axis=dim)


def shards(positions, species, counts):
    lx, ly, lz, width = species.shape
    own = (lx, ly, lz)
    mine = lx * ly * lz
    vmem = pl.BlockSpec(memory_space=pltpu.VMEM)
    block = pl.pallas_call(
        sort_kernel,
        out_shape=jax.ShapeDtypeStruct((lx, ly, lz, 7, width), F32),
        in_specs=[vmem, vmem, pl.BlockSpec(memory_space=pltpu.SMEM)],
        out_specs=vmem,
        name="sort",
    )(positions, species, counts)
    for axis, dim, periodic in (("gx", 0, True), ("gy", 1, True), ("gz", 2, False)):
        block = extended(block, axis, dim, periodic)
    tiles = (lx + 2) * (ly + 2) * (lz + 2)
    cells = (lx + 1) * (ly + 1) * (lz + 1)
    return pl.pallas_call(
        functools.partial(main_kernel, own),
        out_shape=(
            jax.ShapeDtypeStruct((3, lx, ly, lz, width), F32),
            jax.ShapeDtypeStruct((lx, ly, lz, width), F32),
        ),
        in_specs=[vmem],
        out_specs=(vmem, vmem),
        scratch_shapes=[
            pltpu.VMEM((tiles, 8, 128), F32),
            pltpu.VMEM((tiles, 8, 128), jnp.int32),
            pltpu.VMEM((tiles, 8, 128), jnp.int32),
            pltpu.VMEM((tiles, 128, 128), BF16),
            pltpu.VMEM((cells, 8, 128), F32),
            pltpu.VMEM((cells, 8, 8, 128), jnp.int32),
            pltpu.VMEM((cells, 8, 128), F32),
            pltpu.VMEM((cells + tiles, 8, 128), F32),
            pltpu.VMEM((cells, 128), jnp.int32),
            pltpu.VMEM((mine + 1, 8, 128), F32),
            pltpu.VMEM((8, 128), F32),
            pltpu.VMEM((mine, 8, 128), F32),
            pltpu.VMEM((mine, 5, 8, 128), F32),
            pltpu.VMEM((128, 512), BF16),
            pltpu.VMEM((cells, 128, 256), BF16),
            pltpu.VMEM((128, 128), BF16),
            pltpu.VMEM((128, 512), F32),
            pltpu.SMEM((cells, 128), jnp.int32),
            pltpu.SMEM((tiles + 1,), jnp.int32),
            pltpu.SMEM((tiles + 1,), jnp.int32),
            pltpu.SemaphoreType.DMA,
        ],
        compiler_params=pltpu.CompilerParams(vmem_limit_bytes=24 << 20),
        name="atoms",
    )(block.reshape(tiles, 7, width))


def solution(mesh):
    placed = (P(None, "gx", "gy", "gz", None), P("gx", "gy", "gz", None), P("gx", "gy", "gz"))
    return jax.shard_map(
        shards,
        mesh=mesh,
        in_specs=placed,
        out_specs=(P(None, "gx", "gy", "gz", None), P("gx", "gy", "gz", None)),
        check_vma=False,
    )
```

```python
import functools

import jax
import jax.numpy as jnp
from jax import lax
from jax.experimental import pallas as pl
from jax.experimental.pallas import tpu as pltpu
from jax.sharding import PartitionSpec as P

CUTOFF_SQUARED = 0.2025
INVERSE_CUTOFF = 1.0 / 0.45
DENSITY_STEP = 0.4
CUBE_ROOT_STEP = 1.4 ** (1.0 / 3.0) - 1.0
EMBED_STEP = -0.3
LOWEST_LIMIT = 0.4505
HIGHEST_LIMIT = 0.5495
POOL = 32
PAIR_BASE = 0.6
PAIR_STEP = 0.3

F32 = jnp.float32
BF16 = jnp.bfloat16
OCTANTS = [(bx, by, bz) for bx in (0, 1) for by in (0, 1) for bz in (0, 1)]


def rows_iota(shape):
    return lax.broadcasted_iota(jnp.int32, shape, 0)


def lanes_iota(shape):
    return lax.broadcasted_iota(jnp.int32, shape, 1)


def split_three(value):
    first = value.astype(BF16).astype(F32)
    rest = value - first
    second = rest.astype(BF16).astype(F32)
    third = (rest - second).astype(BF16).astype(F32)
    return first, second, third


def left_stack(value):
    one, two, three = split_three(value)
    return jnp.concatenate([one, two, one, two, three, one], axis=0)


def right_stack(value):
    one, two, three = split_three(value)
    return jnp.concatenate([one, one, two, two, one, three], axis=0)


def block_diagonal(first, second):
    depth = first.shape[0]
    zero = jnp.zeros_like(first)
    pad = jnp.zeros((128 - 2 * depth, 256), F32)
    top = jnp.concatenate([first, zero], axis=1)
    low = jnp.concatenate([zero, second], axis=1)
    return jnp.concatenate([top, low, pad], axis=0).astype(BF16)


def row_choice(rows, pairs, other):
    for row, value in pairs:
        other = jnp.where(rows == row, value, other)
    return other


def norm_row(value):
    square = value * value
    return square[0:1] + square[1:2] + square[2:3]


def halves(value, group, limits, order):
    below = jnp.sum(jnp.where(value < limits, group, 0.0), axis=1, keepdims=True)
    total = jnp.sum(group, axis=1, keepdims=True)
    score = jnp.abs(2.0 * below - total) * 8.0 + order
    best = jnp.min(score, axis=0, keepdims=True)
    limit = jnp.max(jnp.where(score == best, limits, 0.0), axis=0, keepdims=True)
    return jnp.where(value >= limit, group, 0.0), jnp.where(value >= limit, 0.0, group)


def sublane_exclusive(value, rows):
    total = value
    for step in (1, 2, 4):
        total = total + jnp.where(rows >= step, pltpu.roll(total, step, 0), 0.0)
    return total - value


def sort_kernel(position_ref, species_ref, count_ref, sorted_ref):
    lx, ly, lz, _ = species_ref.shape
    rows = rows_iota((8, 128))
    wide_rows = rows_iota((128, 128))
    wide_lanes = lanes_iota((128, 128))
    triangle = jnp.where(wide_rows <= wide_lanes, 1.0, 0.0).astype(BF16)
    lane = lanes_iota((1, 128))
    order = rows.astype(F32)
    limits = LOWEST_LIMIT + (HIGHEST_LIMIT - LOWEST_LIMIT) / 7.0 * order
    for x in range(lx):
        for y in range(ly):
            for z in range(lz):
                occupied = jnp.where(lane < count_ref[x, y, z], 1.0, 0.0)
                groups = [jnp.broadcast_to(occupied, (8, 128))]
                for k in range(3):
                    value = jnp.broadcast_to(position_ref[k, x, y, z : z + 1], (8, 128))
                    pairs = [halves(value, group, limits, order) for group in groups]
                    groups = [part for high, low in pairs for part in (low, high)]
                mask = row_choice(rows, list(enumerate(groups))[1:], groups[0])
                octant = jnp.sum(mask * order, axis=0, keepdims=True)
                feature = row_choice(
                    rows,
                    [(k, position_ref[k, x, y, z : z + 1]) for k in range(3)]
                    + [(3, occupied), (4, species_ref[x, y, z : z + 1].astype(F32)), (5, octant)],
                    jnp.zeros((8, 128), F32),
                )
                prefix = jnp.dot(mask.astype(BF16), triangle, preferred_element_type=F32)
                total = jnp.broadcast_to(jnp.sum(mask, axis=1, keepdims=True), (8, 128))
                start = sublane_exclusive(total, rows)
                place = jnp.sum(mask * (prefix - 1.0 + start), axis=0, keepdims=True)
                rank = jnp.where(occupied > 0.5, place.astype(jnp.int32), lane)
                chosen = jnp.where(jnp.broadcast_to(rank, (128, 128)) == wide_rows, 1.0, 0.0).astype(BF16)
                one, two, three = split_three(feature)
                pieces = jnp.concatenate([one, two, three, jnp.zeros_like(one)], axis=0).astype(BF16)
                moved = lax.dot_general(
                    pieces, chosen, (((1,), (1,)), ((), ())), preferred_element_type=F32
                )
                whole = (moved[16:24] + moved[8:16]) + moved[0:8]
                sorted_ref[x, y, z] = row_choice(rows, [(6, rank.astype(F32))], whole)[0:7]


def main_kernel(
    own, ext_ref, force_ref, energy_ref,
    frame_ref, size_ref, start_ref, left_ref, cell_ref, base_ref, dense_ref, dual_ref, count_ref, mine_ref, pool_ref,
    own_ref, acc_ref, pick_ref, wide_ref, spare_ref, spread_ref, table_ref, extra_cell_ref, extra_index_ref, copied,
):
    lx, ly, lz = own
    nx, ny, nz = lx + 2, ly + 2, lz + 2
    cx, cy, cz = lx + 1, ly + 1, lz + 1
    rows = rows_iota((8, 128))
    lane = lanes_iota((8, 128))
    zero = jnp.zeros((8, 128), F32)

    def tile_of(x, y, z):
        return (x * ny + y) * nz + z

    def cell_of(a, b, c):
        return (a * cy + b) * cz + c

    def mine_of(x, y, z):
        return ((x - 1) * ly + (y - 1)) * lz + (z - 1)

    def along(value, source):
        return jnp.take_along_axis(value, source, axis=1, mode="promise_in_bounds")

    def spread_row(ref, index, row):
        return jnp.broadcast_to(ref[index, row : row + 1], (8, 128))

    def right_rows(scaled):
        return row_choice(
            rows, [(3, 1.0 - norm_row(scaled)), (4, -1.0)], jnp.where(rows < 3, 2.0 * scaled, 0.0)
        )

    pick_rows = rows_iota((128, 512))
    pick_group = lanes_iota((128, 512)) // 128
    first_row = jnp.where(pick_group == 3, 51, pick_group)
    chosen = (pick_rows == first_row) | (pick_rows == first_row + 8) | (pick_rows == first_row + 32)
    pick_ref[...] = jnp.where(chosen, 1.0, 0.0).astype(BF16)

    @pl.loop(0, nx)
    def _(x):
        middle = jnp.where(rows == 0, x.astype(F32) - 0.5 * nx, 0.0)
        for y, z in [(y, z) for y in range(ny) for z in range(nz)]:
            tile = tile_of(x, y, z)
            feature = jnp.concatenate([ext_ref[tile], jnp.zeros((1, 128), F32)], axis=0)
            mask = jnp.where(feature[5:6] == rows.astype(F32), feature[3:4], 0.0)
            total = jnp.broadcast_to(jnp.sum(mask, axis=1, keepdims=True), (8, 128))
            size_ref[tile] = total.astype(jnp.int32)
            start_ref[tile] = sublane_exclusive(total, rows).astype(jnp.int32)
            offset = row_choice(rows, [(1, y - 0.5 * ny), (2, z - 0.5 * nz)], middle)
            scaled = (feature + offset) * INVERSE_CUTOFF
            frame_ref[tile] = jnp.where(rows < 3, scaled, feature)
            weight = feature[3:4] * (1.0 + CUBE_ROOT_STEP * feature[4:5])
            left = row_choice(rows, [(3, 1.0), (4, norm_row(scaled))], jnp.where(rows < 3, scaled, 0.0)) * weight
            left_ref[tile] = jnp.concatenate([left_stack(left), jnp.zeros((80, 128), F32)], axis=0).astype(BF16)

    @pl.loop(0, cx)
    def _(a):
        for b, c in [(b, c) for b in range(cy) for c in range(cz)]:
            cell = cell_of(a, b, c)
            base = jnp.zeros((8, 128), jnp.int32)
            packed = zero
            for k, (bx, by, bz) in enumerate(OCTANTS):
                tile = tile_of(a + 1 - bx, b + 1 - by, c + 1 - bz)
                base_ref[cell, k] = base
                moved = along(frame_ref[tile], (lane + (spread_row(start_ref, tile, k) - base)) & 127)
                packed = jnp.where(lane >= base, moved, packed)
                base = base + spread_row(size_ref, tile, k)
            cell_ref[cell] = jnp.where(lane < base, packed, 0.0)
            count_ref[pl.ds(cell, 1)] = base[0:1]

    counting = pltpu.make_async_copy(count_ref, table_ref, copied)
    counting.start()

    def density_of(packed, tiles):
        stack = jnp.concatenate([right_stack(right_rows(packed)), jnp.zeros((80, 128), F32)], axis=0)
        turned = stack.astype(BF16).T
        groups = [zero] * 16
        for k in range(0, 8, 2):
            right = jnp.concatenate([left_ref[tiles[k]], left_ref[tiles[k + 1]]], axis=1)
            reach = jnp.maximum(jnp.dot(turned, right, preferred_element_type=F32), 0.0)
            cube = reach * reach * reach
            for g in range(16):
                part = cube[8 * g : 8 * g + 8]
                groups[g] = groups[g] + part[:, 0:128] + part[:, 128:256]
        both = zero
        for g in range(16):
            total = jnp.sum(groups[g], axis=1, keepdims=True)
            both = jnp.where(lane == rows + 8 * g, total, both)
        occupied, species = packed[3:4], packed[4:5]
        weight = occupied * (1.0 + DENSITY_STEP * species)
        density = jnp.sum(both, axis=0, keepdims=True) - weight
        slope = -0.5 * (occupied * (1.0 + EMBED_STEP * species)) / jnp.sqrt(1.0 + density)
        pair = occupied * (PAIR_BASE + PAIR_STEP * species)
        dual = row_choice(rows, [(3, weight), (4, pair), (5, slope)], packed)
        return jnp.broadcast_to(density, (8, 128)), dual

    for a in range(cx):
        for b, c in [(b, c) for b in range(cy) for c in range(cz)]:
            cell = cell_of(a, b, c)
            tiles = [tile_of(a + 1 - bx, b + 1 - by, c + 1 - bz) for bx, by, bz in OCTANTS]
            dense_ref[cell], dual_ref[cell] = density_of(cell_ref[cell], tiles)

    counting.wait()
    extras = jnp.int32(0)
    most = jnp.int32(0)
    spilled = jnp.int32(0)
    for cell in range(cx * cy * cz):
        count = table_ref[cell, 0]
        extra_cell_ref[extras] = cell
        extra_index_ref[extras] = 1
        extras = extras + (count > 128).astype(jnp.int32)
        most = jnp.maximum(most, count)
        spilled = spilled + jnp.maximum(count - 128, 0)
    for x in range(1, lx + 1):
        for y in range(1, ly + 1):
            for z in range(1, lz + 1):
                tile = tile_of(x, y, z)
                density = zero
                for k, (bx, by, bz) in enumerate(OCTANTS):
                    cell = cell_of(x + bx - 1, y + by - 1, z + bz - 1)
                    start = spread_row(start_ref, tile, k)
                    moved = along(dense_ref[cell], (lane + (base_ref[cell, k] - start)) & 127)
                    density = jnp.where(lane >= start, moved, density)
                mine_ref[mine_of(x, y, z)] = density

    def more(cell, extras):
        def put(index, extras):
            extra_cell_ref[extras] = cell
            extra_index_ref[extras] = index
            return extras + 1

        return lax.fori_loop(2, (table_ref[cell, 0] + 127) // 128, put, extras)

    extras = lax.fori_loop(0, jnp.where(most > 256, cx * cy * cz, 0), more, extras)

    def around(cell):
        a = cell // (cy * cz)
        b = (cell // cz) % cy
        c = cell % cz
        return [(a + 1 - bx, b + 1 - by, c + 1 - bz) for bx, by, bz in OCTANTS]

    def own_tile(x, y, z):
        inside = (x >= 1) & (x <= lx) & (y >= 1) & (y <= ly) & (z >= 1) & (z <= lz)
        return inside, mine_of(x, y, z)

    pooled = spilled <= POOL
    pool_ref[...] = zero

    def extra_density(extra, offset):
        cell, index = extra_cell_ref[extra], extra_index_ref[extra]
        near = around(cell)
        tiles = [tile_of(*place) for place in near]
        packed = zero
        for k, tile in enumerate(tiles):
            place = lane + 128 * index - base_ref[cell, k]
            inside = (place >= 0) & (place < spread_row(size_ref, tile, k))
            moved = along(frame_ref[tile], (place + spread_row(start_ref, tile, k)) & 127)
            packed = jnp.where(inside, moved, packed)
        density, dual = density_of(packed, tiles)
        dual_ref[cx * cy * cz + extra] = dual
        held = jnp.minimum(table_ref[cell, 0] - 128 * index, 128)
        placed = (lane >= offset) & (lane < offset + held) & pooled
        pool_ref[...] = jnp.where(placed, along(dual, (lane - offset) & 127), pool_ref[...])
        for k, tile in enumerate(tiles):
            inside, mine = own_tile(*near[k])
            mine = jnp.where(inside, mine, lx * ly * lz)
            local = lane - spread_row(start_ref, tile, k)
            place = local + base_ref[cell, k] - 128 * index
            keep = (local >= 0) & (local < spread_row(size_ref, tile, k)) & (place >= 0) & (place < 128)
            mine_ref[mine] = jnp.where(keep, along(density, place & 127), mine_ref[mine])
        return offset + held

    lax.fori_loop(0, extras, extra_density, jnp.int32(0))

    def force_stacks(packed):
        pair = packed[4:5]
        left = row_choice(rows, [(3, 1.0), (4, norm_row(packed))], jnp.where(rows < 3, packed, 0.0))
        other = row_choice(rows, [(5, packed[3:4]), (6, packed[5:6])], left * pair)
        return left_stack(left), left_stack(other)

    def force_left(packed):
        full = jnp.concatenate([*force_stacks(packed), jnp.zeros((32, 128), F32)], axis=0)
        return full.astype(BF16).T

    def spread_of(wide):
        return jnp.dot(wide, pick_ref[...], preferred_element_type=F32)

    def own_stacks(feature):
        right = right_rows(feature)
        mixed = row_choice(
            rows, [(5, feature[5:6]), (6, feature[3:4])], right * ((4.0 / 3.0) * feature[4:5])
        )
        return right_stack(right), right_stack(mixed)

    def add_terms(sums, reach, other, spreads):
        reach = jnp.maximum(reach, 0.0)
        square = reach * reach
        coef = square * other
        for axis in range(3):
            sums[axis] = sums[axis] + coef * spreads[axis]
        sums[3] = sums[3] + square * square * spreads[3]
        sums[4] = sums[4] + coef

    def spare_sums(size, right, sums):
        sums = list(sums)
        both = jnp.dot(spare_ref[0:size], right, preferred_element_type=F32)
        for part in range(size // 8):
            span = slice(8 * part, 8 * part + 8)
            spreads = [spread_ref[span, 128 * k : 128 * k + 128] for k in range(4)]
            add_terms(sums, both[span, 0:128], both[span, 128:256], spreads)
        return sums

    def cell_sums(slots, turned, half):
        groups = [[zero] * 5 for _ in range(4)]
        for slot in slots:
            both = jnp.dot(turned[32 * half : 32 * half + 32], wide_ref[slot], preferred_element_type=F32)
            spreads = [spread_row(dual_ref, slot, k) for k in (0, 1, 2, 4)]
            for g in range(4):
                part = both[8 * g : 8 * g + 8]
                add_terms(groups[g], part[:, 0:128], part[:, 128:256], spreads)
        return groups

    @pl.loop(0, cx)
    def _(a):
        for k in range(cy * cz):
            cell = a * (cy * cz) + k
            wide_ref[cell] = block_diagonal(*force_stacks(dual_ref[cell]))

    pool_wide = force_left(pool_ref[...])
    spare_ref[...] = pool_wide
    spread_ref[0:POOL] = spread_of(pool_wide[0:POOL])

    for x in range(1, lx + 1):
        for y, z in [(y, z) for y in range(1, ly + 1) for z in range(1, lz + 1)]:
            mine = mine_of(x, y, z)
            feature = frame_ref[tile_of(x, y, z)]
            occupied, species = feature[3:4], feature[4:5]
            strength = occupied * (1.0 + EMBED_STEP * species)
            root = jnp.sqrt(1.0 + mine_ref[mine][0:1])
            feature = row_choice(
                rows,
                [
                    (3, occupied * (1.0 + DENSITY_STEP * species)),
                    (4, occupied * (PAIR_BASE + PAIR_STEP * species)),
                    (5, -0.5 * strength / root),
                    (6, -strength * root),
                ],
                feature,
            )
            own_ref[mine] = feature
            stacks = own_stacks(feature)
            turned = jnp.concatenate([*stacks, jnp.zeros((32, 128), F32)], axis=0).astype(BF16).T
            slots = [cell_of(x + bx - 1, y + by - 1, z + bz - 1) for bx, by, bz in OCTANTS]
            sums = spare_sums(POOL, block_diagonal(*stacks), [zero] * 5)
            found = [zero] * 5
            for half in range(4):
                for g, group in enumerate(cell_sums(slots, turned, half)):
                    spot = lane == rows + (32 * half + 8 * g)
                    for k in range(5):
                        found[k] = jnp.where(spot, jnp.sum(group[k], axis=1, keepdims=True), found[k])
            for k in range(5):
                acc_ref[mine, k] = sums[k] + found[k]

    @pl.loop(0, jnp.where(pooled, 0, extras))
    def _(extra):
        near = around(extra_cell_ref[extra])
        spare_ref[...] = force_left(dual_ref[cx * cy * cz + extra])
        spread_ref[...] = spread_of(spare_ref[...])
        for place in near:
            inside, mine = own_tile(*place)

            @pl.when(inside)
            def _():
                right = block_diagonal(*own_stacks(own_ref[mine]))
                sums = spare_sums(128, right, [acc_ref[mine, k] for k in range(5)])
                for k in range(5):
                    acc_ref[mine, k] = sums[k]

    for x in range(lx):
        for y in range(ly):
            for z in range(lz):
                mine = (x * ly + y) * lz + z
                feature = own_ref[mine]
                parts = [jnp.sum(acc_ref[mine, k], axis=0, keepdims=True) for k in range(5)]
                pair = feature[4:5]
                energy = feature[6:7] + 0.5 * pair * (parts[3] - pair)
                scale = -6.0 / (CUTOFF_SQUARED * INVERSE_CUTOFF)
                result = row_choice(
                    rows,
                    [(k, (parts[k] - feature[k : k + 1] * parts[4]) * scale) for k in range(3)],
                    jnp.broadcast_to(energy, (8, 128)),
                )
                rank = ext_ref[tile_of(x + 1, y + 1, z + 1), 6:7].astype(jnp.int32)
                result = along(result, jnp.broadcast_to(rank, (8, 128)))
                for axis in range(3):
                    force_ref[axis, x, y, z : z + 1] = result[axis : axis + 1]
                energy_ref[x, y, z : z + 1] = result[3:4]


def extended(block, axis, dim, periodic):
    count = lax.axis_size(axis)
    size = block.shape[dim]
    first = lax.slice_in_dim(block, 0, 1, axis=dim)
    last = lax.slice_in_dim(block, size - 1, size, axis=dim)
    if periodic and count == 2 and size == 2:
        other = lax.ppermute(block, axis, [(0, 1), (1, 0)])
        low = lax.slice_in_dim(other, 1, 2, axis=dim)
        high = lax.slice_in_dim(other, 0, 1, axis=dim)
    elif count % 2 == 0:
        place = lax.axis_index(axis)
        even = place % 2 == 0
        inner = [(i, i ^ 1) for i in range(count)]
        outer = [(i, (i - 1 if i % 2 == 0 else i + 1) % count) for i in range(count)]
        if not periodic:
            outer[0], outer[-1] = (0, 0), (count - 1, count - 1)
        near = lax.ppermute(jnp.where(even, last, first), axis, inner)
        far = lax.ppermute(jnp.where(even, first, last), axis, outer)
        if not periodic:
            far = jnp.where((place == 0) | (place == count - 1), 0.0, far)
        low, high = jnp.where(even, far, near), jnp.where(even, near, far)
    else:
        forward = [(i, i + 1) for i in range(count - 1)]
        if periodic:
            forward.append((count - 1, 0))
        backward = [(target, source) for source, target in forward]
        low = lax.ppermute(last, axis, forward)
        high = lax.ppermute(first, axis, backward)
    return jnp.concatenate([low, block, high], axis=dim)


def shards(positions, species, counts):
    lx, ly, lz, width = species.shape
    own = (lx, ly, lz)
    mine = lx * ly * lz
    vmem = pl.BlockSpec(memory_space=pltpu.VMEM)
    block = pl.pallas_call(
        sort_kernel,
        out_shape=jax.ShapeDtypeStruct((lx, ly, lz, 7, width), F32),
        in_specs=[vmem, vmem, pl.BlockSpec(memory_space=pltpu.SMEM)],
        out_specs=vmem,
        name="sort",
    )(positions, species, counts)
    for axis, dim, periodic in (("gx", 0, True), ("gy", 1, True), ("gz", 2, False)):
        block = extended(block, axis, dim, periodic)
    tiles = (lx + 2) * (ly + 2) * (lz + 2)
    cells = (lx + 1) * (ly + 1) * (lz + 1)
    return pl.pallas_call(
        functools.partial(main_kernel, own),
        out_shape=(
            jax.ShapeDtypeStruct((3, lx, ly, lz, width), F32),
            jax.ShapeDtypeStruct((lx, ly, lz, width), F32),
        ),
        in_specs=[vmem],
        out_specs=(vmem, vmem),
        scratch_shapes=[
            pltpu.VMEM((tiles, 8, 128), F32),
            pltpu.VMEM((tiles, 8, 128), jnp.int32),
            pltpu.VMEM((tiles, 8, 128), jnp.int32),
            pltpu.VMEM((tiles, 128, 128), BF16),
            pltpu.VMEM((cells, 8, 128), F32),
            pltpu.VMEM((cells, 8, 8, 128), jnp.int32),
            pltpu.VMEM((cells, 8, 128), F32),
            pltpu.VMEM((cells + tiles, 8, 128), F32),
            pltpu.VMEM((cells, 128), jnp.int32),
            pltpu.VMEM((mine + 1, 8, 128), F32),
            pltpu.VMEM((8, 128), F32),
            pltpu.VMEM((mine, 8, 128), F32),
            pltpu.VMEM((mine, 5, 8, 128), F32),
            pltpu.VMEM((128, 512), BF16),
            pltpu.VMEM((cells, 128, 256), BF16),
            pltpu.VMEM((128, 128), BF16),
            pltpu.VMEM((128, 512), F32),
            pltpu.SMEM((cells, 128), jnp.int32),
            pltpu.SMEM((tiles + 1,), jnp.int32),
            pltpu.SMEM((tiles + 1,), jnp.int32),
            pltpu.SemaphoreType.DMA,
        ],
        compiler_params=pltpu.CompilerParams(vmem_limit_bytes=24 << 20),
        name="atoms",
    )(block.reshape(tiles, 7, width))


def solution(mesh):
    placed = (P(None, "gx", "gy", "gz", None), P("gx", "gy", "gz", None), P("gx", "gy", "gz"))
    return jax.shard_map(
        shards,
        mesh=mesh,
        in_specs=placed,
        out_specs=(P(None, "gx", "gy", "gz", None), P("gx", "gy", "gz", None)),
        check_vma=False,
    )
```
